128 devices in a mesh: inner: 8 (over z, core), outer: 16 (over x, y).
Axes of the slice: x: 4, y: 4, z: 4, core: 2. Of those that a mesh axis runs over, the one named last changes fastest.
Arguments:
- inner_state: float32 [2, 32, 2048], P(None, 'inner', 'outer'), may hold values from -6 to 6
- outer_state: float32 [2, 1280, 8192], P(None, 'inner', 'outer'), may hold values from -6 to 6
- energies: float32 [32, 2048], P('inner', 'outer'), may hold values from -2 to 2
- dipole: float32 [32, 2048, 2048], P('inner', 'outer'), may hold values from -0.125 to 0.125
- surface: float32 [32, 40, 2048], P('inner', None, 'outer'), may hold values from -0.125 to 0.125
- thresholds: float32 [1280], P('inner'), may hold values from 0 to 2
- coupling_coef: float32 [32, 40, 40], P('inner'), may hold values from -1 to 1
- coupling_pattern: int32 [32, 40, 40], P('inner'), may hold values 0 or 1
- block_sizes: int32 [32], P('inner'), may hold values from 1 to 2048, 61440 in all
- field_strength: float32 [2], replicated, may hold values from 0.5 to 2
Outputs:
- inner_final: float32 [2, 32, 2048], P(None, 'inner', 'outer')
- outer_final: float32 [2, 1280, 8192], P(None, 'inner', 'outer')
The draws below stay inside these ranges and needn't reach their ends.
All inputs are finite; a program needn't handle non-finite values. No bound on the sum of `coupling_pattern` or of `block_sizes` on one device may be relied on, other than what follows from the above.
Results may differ from the reference program's by a relative error of at most 0.0001.
Values sent between devices are 32-bit elements; how exact they have to be, the bound alone decides.
No kernel may reach another device: no remote copies, remote signals or barrier semaphores. Data moves between devices by JAX's collectives and lax.ppermute only.
A program may use at most 128 MiB of HBM per device.

```python
import math
import jax
import jax.numpy as jnp
import numpy as np
from jax import lax

BMAX = 2048
CHL = 40
STEPS = 2
ORDER = 4
NL = 32
NC = 1280
NR = 8192


def touch_ends(entries, key, low, high):
    longest = entries.shape.index(max(entries.shape))
    spots = []
    for shift in (0, 1):
        where = [jax.random.randint(jax.random.fold_in(key, axis), (), 0, length) for axis, length in enumerate(entries.shape)]
        where[longest] = (where[longest] + shift) % entries.shape[longest]
        spots.append(tuple(where))
    return entries.at[spots[0]].set(low).at[spots[1]].set(high)


def shard_levels(rng, extent, split, least, largest):
    factor_of, own = 1.0, jax.random.fold_in(rng, 6)
    for position, parts in split:
        draws = jnp.exp(jax.random.uniform(jax.random.fold_in(own, position), (parts,), jnp.float32, least / len(split), largest / len(split)))
        factor_of = factor_of * jnp.repeat(draws, extent[position] // parts).reshape([-1 if axis == position else 1 for axis in range(len(extent))])
    return factor_of


def length_profile(amount, total, reach, lean):
    loads = [(1 << 20) // math.isqrt(rank ** lean) + 1 for rank in range(2, amount + 1)]
    surplus, given = total - reach - (amount - 1), [1] * (amount - 1)
    while surplus > 0:
        free = [i for i in range(amount - 1) if given[i] < reach]
        whole, left = sum([loads[i] for i in free]), surplus
        for i in free:
            addition = min(reach - given[i], max(1, left * loads[i] // whole), surplus)
            given[i] = given[i] + addition
            surplus = surplus - addition
    return np.array([reach] + given)


def ragged(stream_key, amount, total, reach, slope):
    if amount == 2:
        one = jax.random.randint(stream_key, (), max(1, total - reach), min(reach, total - 1) + 1)
        return jnp.stack([one, total - one])
    sizes = jnp.asarray(length_profile(amount, total, reach, slope), jnp.int32)
    pairs = (amount - 1) // 2
    giver, taker = sizes[1:1 + 2 * pairs:2], sizes[2:2 + 2 * pairs:2]
    room = jnp.minimum(giver - 1, reach - taker)
    shifted = jax.random.randint(jax.random.fold_in(stream_key, 1), (pairs,), 0, 1 << 20) % (room + 1)
    sizes = sizes.at[1:1 + 2 * pairs:2].set(giver - shifted).at[2:2 + 2 * pairs:2].set(taker + shifted)
    return sizes[jax.random.permutation(jax.random.fold_in(stream_key, 2), amount)]


def bell_draw(stream_key, shape, width, limit, split=(), held_as=jnp.bfloat16):
    result = width * jax.random.normal(stream_key, shape, jnp.float32)
    if split:
        result = result * shard_levels(stream_key, shape, split, -0.22, 0.18)
    return jnp.clip(result, -limit, limit).astype(held_as)


def setup_inputs(seed: int = 0) -> dict:
    streams_of = jax.random.split(jax.random.key(seed), 11)
    inner_state = bell_draw(streams_of[0], (2, NL, BMAX), 1.0, 6.0, ((1, 8), (2, 16)), jnp.float32)
    outer_state = bell_draw(streams_of[1], (2, NC, NR), 1.0, 6.0, ((1, 8), (2, 16)), jnp.float32)
    energies = jnp.clip(jax.random.uniform(streams_of[2], (NL, BMAX), jnp.float32, -2.0, 2.0) * shard_levels(streams_of[2], (NL, BMAX), ((0, 8), (1, 16)), -0.4, 0.0), -2.0, 2.0)
    dipole = bell_draw(streams_of[3], (NL, BMAX, BMAX), BMAX ** -0.5, 0.125, ((0, 8), (1, 16)), jnp.float32)
    surface = bell_draw(streams_of[4], (NL, CHL, BMAX), BMAX ** -0.5, 0.125, ((0, 8), (2, 16)), jnp.float32)
    thresholds = jnp.clip(2.0 * jax.random.uniform(streams_of[5], (NC,), jnp.float32) ** shard_levels(streams_of[5], (NC,), ((0, 8),), -0.2, 0.2), 0.0, 2.0)
    coupling_coef = bell_draw(streams_of[6], (NL, CHL, CHL), CHL ** -0.5, 1.0, ((0, 8),), jnp.float32)
    coupling_pattern = touch_ends((jax.random.randint(streams_of[7], (NL, CHL, CHL), 0, 2) < 1).astype(jnp.int32), jax.random.fold_in(streams_of[7], 1), 0, 1)
    block_sizes = ragged(streams_of[8], NL, NL * BMAX * 15 // 16, BMAX, 2).astype(jnp.int32)
    field_strength = jnp.clip(jax.random.uniform(streams_of[9], (STEPS,), jnp.float32, 0.5, 2.0), 0.5, 2.0)
    return dict(inner_state=inner_state, outer_state=outer_state, energies=energies, dipole=dipole, surface=surface, thresholds=thresholds, coupling_coef=coupling_coef, coupling_pattern=coupling_pattern, block_sizes=block_sizes, field_strength=field_strength)


kinetic_scale = 3.125
time_step = 0.1


def apply_operator(inner_part, outer_part, live_rows, energies, dipole, surface, thresholds, coupling, strength):
    highest = lax.Precision.HIGHEST
    forward = jnp.einsum('lij,plj->pli', dipole[:-1], inner_part[:, 1:], precision=highest)
    backward = jnp.einsum('lji,plj->pli', dipole[:-1], inner_part[:, :-1], precision=highest)
    zero_block = jnp.zeros((2, 1, BMAX), jnp.float32)
    forward = jnp.concatenate([forward, zero_block], axis=1)
    backward = jnp.concatenate([zero_block, backward], axis=1)
    first_point = outer_part[:, :, 0].reshape(2, NL, CHL)
    surf_term = jnp.einsum('lcs,plc->pls', surface, first_point, precision=highest)
    inner_image = live_rows * (energies * inner_part + strength * (forward + backward) - kinetic_scale * surf_term)
    boundary = jnp.einsum('lcs,pls->plc', surface, inner_part, precision=highest).reshape(2, NC)
    zero_col = jnp.zeros((2, NC, 1), jnp.float32)
    left_cells = jnp.concatenate([boundary[:, :, None], outer_part[:, :, :-1]], axis=2)
    right_cells = jnp.concatenate([outer_part[:, :, 1:], zero_col], axis=2)
    kinetic = kinetic_scale * (2.0 * outer_part - left_cells - right_cells)
    channel_grid = outer_part.reshape(2, NL, CHL, NR)
    upward = jnp.einsum('lab,plbr->plar', coupling[:-1], channel_grid[:, 1:], precision=highest)
    downward = jnp.einsum('lba,plbr->plar', coupling[:-1], channel_grid[:, :-1], precision=highest)
    zero_grid = jnp.zeros((2, 1, CHL, NR), jnp.float32)
    upward = jnp.concatenate([upward, zero_grid], axis=1)
    downward = jnp.concatenate([zero_grid, downward], axis=1)
    outer_image = kinetic + thresholds[None, :, None] * outer_part + strength * (upward + downward).reshape(2, NC, NR)
    return inner_image, outer_image


def reference(inner_state, outer_state, energies, dipole, surface, thresholds, coupling_coef, coupling_pattern, block_sizes, field_strength):
    positions = jnp.arange(BMAX, dtype=jnp.int32)
    live_rows = (positions[None, :] < block_sizes[:, None]).astype(jnp.float32)
    coupling = coupling_coef * coupling_pattern.astype(jnp.float32)
    current = (inner_state * live_rows, outer_state)
    for time_index in range(STEPS):
        strength = field_strength[time_index]
        taylor_term = current
        accumulated = current
        for power in range(1, ORDER + 1):
            inner_image, outer_image = apply_operator(taylor_term[0], taylor_term[1], live_rows, energies, dipole, surface, thresholds, coupling, strength)
            factor = time_step / power
            taylor_term = (factor * jnp.stack([inner_image[1], -inner_image[0]]), factor * jnp.stack([outer_image[1], -outer_image[0]]))
            accumulated = (accumulated[0] + taylor_term[0], accumulated[1] + taylor_term[1])
        current = accumulated
    return current[0], current[1]
```

```python
import functools

import jax
import jax.numpy as jnp
from jax import lax
from jax.experimental import pallas as pl
from jax.experimental.pallas import tpu as pltpu
from jax.sharding import PartitionSpec as P

STEPS = 2
ORDER = 4
kinetic_scale = 3.125
time_step = 0.1

F32 = jnp.float32
BF16 = jnp.bfloat16
HIGHEST = lax.Precision.HIGHEST
VM = pl.BlockSpec(memory_space=pltpu.VMEM)
SM = pl.BlockSpec(memory_space=pltpu.SMEM)

LB = 4
CH = 40
OWN = LB * CH
PTS = 16
HALO = 8
WIDTH = 640
EDGE = 64 + OWN
NT = (((1,), (1,)), ((), ()))


def sds(*shape):
    return jax.ShapeDtypeStruct(shape, F32)


def call(kernel, outs, smem=1, scratch=(), limit=48):
    def run(*args):
        return pl.pallas_call(
            kernel,
            out_shape=outs,
            in_specs=[SM] * smem + [VM] * (len(args) - smem),
            out_specs=[VM] * len(outs),
            scratch_shapes=list(scratch),
            compiler_params=pltpu.CompilerParams(vmem_limit_bytes=limit << 20),
        )(*args)

    return run


def rows_of(lines, shape):
    return lax.broadcasted_iota(jnp.int32, shape, lines)


def block_mask():
    lanes = rows_of(1, (8, 256))
    first = (rows_of(0, (8, 256)) % LB) * CH
    return jnp.where((lanes >= first) & (lanes < first + CH), 1.0, 0.0).astype(F32)


def edge_tiles(strip):
    lanes = rows_of(1, (2 * PTS, 128))
    up = pltpu.roll(strip, 80, 1)[:, 128:]
    down = pltpu.roll(strip, 160, 1)[:, 128:]
    zero = jnp.zeros_like(up)
    up = jnp.where((lanes >= 72) & (lanes < 112), up, zero)
    down = jnp.where((lanes >= 32) & (lanes < 72), down, zero)
    return up, down


def emit(parity, c, strip, dipole, surface, q_ref, a_ref, b_ref, up_ref, down_ref):
    for s in range(16):
        q_ref[s, 0:8, :] = jnp.zeros((8, 128), F32)
    ahead = jnp.concatenate([c[1:4], c[0:1], c[5:8], c[4:5]], axis=0)
    partial = lax.dot_general(c, surface[...], NT, precision=HIGHEST, preferred_element_type=F32)
    partial = partial * block_mask()
    b_re = jnp.sum(partial[0:4], axis=0, keepdims=True)
    b_im = jnp.sum(partial[4:8], axis=0, keepdims=True)
    tail = jnp.concatenate(
        [b_re[:, :128], b_re[:, 128:], b_im[:, :128], b_im[:, 128:], jnp.zeros((4, 128), F32)], axis=0
    )
    for s in range(16):
        q_ref[s, 0:8, :] = ahead
        q_ref[s, 8:16, :] = jnp.zeros((8, 128), F32)
        q_ref[s, 16:24, :] = tail
    for l in range(LB):
        re = jnp.broadcast_to(c[l : l + 1], (128, 128)).T
        im = jnp.broadcast_to(c[4 + l : 5 + l], (128, 128)).T

        def body(s, carry):
            tile = dipole[l, :, pl.ds(pl.multiple_of(s * 128, 128), 128)]
            sum_re = jnp.sum(tile * re, axis=0, keepdims=True)
            sum_im = jnp.sum(tile * im, axis=0, keepdims=True)
            if l < LB - 1:
                q_ref[s, 9 + l : 10 + l, :] = sum_re
                q_ref[s, 13 + l : 14 + l, :] = sum_im
            else:
                up_ref[pl.ds(s, 1), :] = sum_re
                up_ref[pl.ds(16 + s, 1), :] = sum_im
            return carry

        lax.fori_loop(0, 16, body, 0, unroll=4)
    up, down = edge_tiles(strip)
    up_ref[32:64, :] = up
    down_ref[0:8, :] = c
    down_ref[8:32, :] = jnp.zeros((24, 128), F32)
    down_ref[32:64, :] = down

    @pl.when(parity == 0)
    def _():
        a_ref[0:64, :] = up_ref[...]
        b_ref[0:64, :] = down_ref[...]

    @pl.when(parity != 0)
    def _():
        a_ref[0:64, :] = down_ref[...]
        b_ref[0:64, :] = up_ref[...]


def first_kernel(where, inner, live, strip, dipole, surface, pack, c_ref, q_ref, a_ref, b_ref, up_ref, down_ref):
    c = inner[...] * live[...]
    c_ref[...] = c
    a_ref[64:EDGE, :] = pack[...]
    b_ref[64:EDGE, :] = pack[...]
    emit(where[0], c, strip[...], dipole, surface, q_ref, a_ref, b_ref, up_ref, down_ref)


def received(parity, a, b):
    flag = jnp.full(a.shape, parity, jnp.int32) == 0
    return jnp.where(flag, b, a), jnp.where(flag, a, b)


def assemble_kernel(first, where, *refs):
    if first:
        q, a, b, strip, out_ref, low_ref, high_ref = refs
    else:
        q, a, b, out_ref, ghost_ref = refs
    up, down = received(where[0], a[...], b[...])
    out_ref[:, 0:24, :] = q[...]
    for s in range(16):
        out_ref[s, 3:4, :] = down[0:1]
        out_ref[s, 7:8, :] = down[4:5]
        out_ref[s, 8:9, :] = up[s : s + 1]
        out_ref[s, 12:13, :] = up[16 + s : 17 + s]
    ghost = up[32:64] + down[32:64]
    if first:
        whole = strip[...]
        near, far = whole[:, :128], whole[:, 128:] + ghost
        for s in range(16):
            out_ref[s, 24:56, :] = near
            out_ref[s, 56:88, :] = far
        low_ref[...] = up[64:EDGE]
        high_ref[...] = down[64:EDGE]
    else:
        ghost_ref[...] = ghost


def advance(first, last_power, factor, field, dipole, surface, levels, pairs, thresholds, arrived, cs, fs, ghost):
    sums = []
    for l in range(LB):

        def body(s, carry):
            tile = dipole[l, :, pl.ds(pl.multiple_of(s * 128, 128), 128)]
            return (
                carry[0] + tile * arrived[s, l : l + 1, :],
                carry[1] + tile * arrived[s, 4 + l : 5 + l, :],
            )

        zero = jnp.zeros((128, 128), F32)
        re, im = lax.fori_loop(0, 16, body, (zero, zero), unroll=4)
        sums.append((jnp.sum(re.T, axis=0, keepdims=True), jnp.sum(im.T, axis=0, keepdims=True)))
    forward = jnp.concatenate([a for a, _ in sums] + [b for _, b in sums], axis=0)
    backward = arrived[0, 8:16, :]
    tail = arrived[0, 16:24, :]
    for s in range(1, 16):
        backward = backward + arrived[s, 8:16, :]
        tail = tail + arrived[s, 16:24, :]
    lanes = rows_of(1, (2 * PTS, 256))
    if first:
        whole = jnp.concatenate([arrived[0, 24:56, :], arrived[0, 56:88, :]], axis=1)
        own = jnp.where(lanes < OWN, whole, 0.0)
        strip_sum = own
    else:
        own = fs[0:32, :]
        strip_sum = fs[32:64, :]
        whole = jnp.concatenate([own[:, :128], own[:, 128:] + ghost[...]], axis=1)
    c = cs[0:8, :]
    c_sum = c if first else cs[8:16, :]
    edge = jnp.concatenate(
        [jnp.broadcast_to(own[0:1], (4, 256)), jnp.broadcast_to(own[PTS : PTS + 1], (4, 256))], axis=0
    )
    surf = jnp.dot(edge * block_mask(), surface[...], precision=HIGHEST, preferred_element_type=F32)
    image = levels[8:16, :] * (levels[0:8, :] * c + field * (forward + backward) - kinetic_scale * surf)
    c_new = jnp.concatenate([factor * image[4:8], -factor * image[0:4]], axis=0)
    coupled = lax.dot_general(whole, pairs[...], NT, precision=HIGHEST, preferred_element_type=F32)
    b_re = jnp.concatenate([tail[0:1], tail[1:2]], axis=1)
    b_im = jnp.concatenate([tail[2:3], tail[3:4]], axis=1)
    points = rows_of(0, (2 * PTS, 256))
    left = pltpu.roll(own, 1, 0)
    left = jnp.where(points == 0, b_re, jnp.where(points == PTS, b_im, left))
    right = pltpu.roll(own, 2 * PTS - 1, 0)
    right = jnp.where((points == PTS - 1) | (points == 2 * PTS - 1), 0.0, right)
    grid = kinetic_scale * (2.0 * own - left - right) + thresholds[...] * own + field * coupled
    grid = jnp.where(lanes < OWN, grid, 0.0)
    f_new = jnp.concatenate([factor * grid[PTS:], -factor * grid[:PTS]], axis=0)
    c_sum = c_sum + c_new
    strip_sum = strip_sum + f_new
    if last_power:
        return c_sum, c_sum, strip_sum, strip_sum
    return c_new, c_sum, f_new, strip_sum


def middle_kernel(first, last_power, factor, step, where, strengths, *refs):
    dipole, surface, levels, pairs, thresholds, arrived, cs = refs[:7]
    rest = refs[7:]
    fs = ghost = None
    if not first:
        fs, ghost = rest[:2]
        rest = rest[2:]
    cs_ref, fs_ref, q_ref, a_ref, b_ref, up_ref, down_ref = rest
    c, c_sum, f, f_sum = advance(
        first, last_power, factor, strengths[step], dipole, surface, levels, pairs, thresholds, arrived, cs, fs, ghost
    )
    cs_ref[0:8, :] = c
    cs_ref[8:16, :] = c_sum
    fs_ref[0:32, :] = f
    fs_ref[32:64, :] = f_sum
    emit(where[0], c, f, dipole, surface, q_ref, a_ref, b_ref, up_ref, down_ref)


def last_kernel(
    factor, step, where, strengths, dipole, surface, levels, pairs, thresholds, arrived, cs, fs, ghost, bulk, c_ref, out_ref
):
    _, c_sum, _, f_sum = advance(
        False, True, factor, strengths[step], dipole, surface, levels, pairs, thresholds, arrived, cs, fs, ghost
    )
    c_ref[...] = c_sum
    lanes = rows_of(1, (OWN, 128))
    low = jnp.full((OWN, 128), where[1], jnp.int32) == 0
    fixed = (lanes < HALO) & low
    for part in range(2):
        corner = f_sum[part * PTS : (part + 1) * PTS]
        corner = jnp.concatenate([corner, jnp.zeros((128 - PTS, 256), F32)], axis=0).T[:OWN]
        base = part * WIDTH
        out_ref[part, :, 0:128] = jnp.where(fixed, corner, bulk[:, base : base + 128])
        out_ref[part, :, 128:512] = bulk[:, base + 128 : base + 512]


def window_kernel(outer, left, right, out_ref):
    lanes = rows_of(1, (OWN, 128))
    for part in range(2):
        base = part * WIDTH
        out_ref[:, base : base + 512] = outer[part]
        out_ref[:, base + 512 : base + WIDTH] = jnp.where(
            lanes < HALO, right[part], jnp.where(lanes >= 128 - HALO, left[part], 0.0)
        )


GROUPS = ((160, 320, 120, 360), (40, 160, 0, 200), (320, 440, 280, 480))


def bulk_kernel(step, powers, begin, where, strengths, *refs):
    if begin:
        low, own, high, couplings, pack, win_ref, sum_ref, old_ref = refs
        old_ref[0:160, :] = low[...]
        old_ref[160:320, :] = own[...]
        old_ref[320:480, :] = high[...]
        sum_ref[...] = own[...]
    else:
        given, given_sum, couplings, pack, sum_ref, old_ref, win_ref = refs
        old_ref[...] = given[...]
        sum_ref[...] = given_sum[...]
    field = strengths[step]
    lanes = rows_of(1, (1, WIDTH))
    past = (lanes >= 512) & (lanes < 512 + 64) & (jnp.full((1, WIDTH), where[1], jnp.int32) == 15)
    keep = jnp.where(past, 0.0, 1.0).astype(F32)
    source, target = old_ref, win_ref
    for power in powers:
        factor = time_step / power
        for out0, out1, in0, in1 in GROUPS if power < ORDER else GROUPS[:1]:
            matrix = couplings[out0:out1, in0:in1]
            m_hi = matrix.astype(BF16)
            m_lo = (matrix - m_hi.astype(F32)).astype(BF16)
            images = []
            for part in range(2):
                cols = slice(part * WIDTH, (part + 1) * WIDTH)
                f = source[in0:in1, cols]
                f_hi = f.astype(BF16)
                f_lo = (f - f_hi.astype(F32)).astype(BF16)
                coupled = jnp.dot(m_hi, f_hi, preferred_element_type=F32)
                coupled = coupled + jnp.dot(m_hi, f_lo, preferred_element_type=F32)
                coupled = coupled + jnp.dot(m_lo, f_hi, preferred_element_type=F32)
                own = source[out0:out1, cols]
                left = pltpu.roll(own, 1, 1)
                right = pltpu.roll(own, WIDTH - 1, 1)
                level = pack[out0:out1, CH : CH + 1]
                image = kinetic_scale * (2.0 * own - left - right) + level * own + field * coupled
                images.append(image * keep)
            new_re = factor * images[1]
            new_im = -factor * images[0]
            target[out0:out1, 0:WIDTH] = new_re
            target[out0:out1, WIDTH : 2 * WIDTH] = new_im
            if out0 == 160:
                sum_ref[:, 0:WIDTH] = sum_ref[:, 0:WIDTH] + new_re
                sum_ref[:, WIDTH : 2 * WIDTH] = sum_ref[:, WIDTH : 2 * WIDTH] + new_im
        if power == powers[0]:
            target[0:40, :] = source[0:40, :]
            target[440:480, :] = source[440:480, :]
        source, target = target, source
    if begin and source is not win_ref:
        win_ref[...] = old_ref[...]


def pair_up(lower, upper):
    return [(a, b) for a, b in zip(lower, upper)] + [(b, a) for a, b in zip(lower, upper)]


def coupling_matrix(blocks):
    count = blocks.shape[0]
    up = blocks[:, :, None, :]
    before = jnp.concatenate([jnp.zeros_like(blocks[:1]), blocks[:-1]], axis=0)
    down = jnp.swapaxes(before, 1, 2)[:, :, None, :]
    here = jnp.arange(count)[:, None, None, None]
    there = jnp.arange(count)[None, None, :, None]
    whole = jnp.where(there == here + 1, up, 0.0) + jnp.where(there == here - 1, down, 0.0)
    return whole.reshape(count * CH, count * CH)


def local(
    inner_state,
    outer_state,
    energies,
    dipole,
    surface,
    thresholds,
    coupling_coef,
    coupling_pattern,
    block_sizes,
    field_strength,
):
    inner_count = lax.axis_size("inner")
    outer_count = lax.axis_size("outer")
    i = lax.axis_index("inner")
    o = lax.axis_index("outer")
    where = jnp.stack([i % 2, o]).astype(jnp.int32)
    swap = pair_up(range(0, inner_count, 2), range(1, inner_count, 2))
    chips = pair_up(range(1, inner_count - 1, 2), range(2, inner_count, 2))
    even = pair_up(range(0, outer_count, 2), range(1, outer_count, 2))
    odd = pair_up(range(1, outer_count - 1, 2), range(2, outer_count, 2))

    rows = o * 128 + jnp.arange(128, dtype=jnp.int32)
    live = (rows[None, :] < block_sizes[:, None]).astype(F32)
    live = jnp.concatenate([live, live], axis=0)
    levels = jnp.concatenate([energies, energies, live], axis=0)
    coupling = coupling_coef * coupling_pattern.astype(F32)
    has_next = (i * LB + jnp.arange(LB) < inner_count * LB - 1).astype(F32)
    coupling = coupling * has_next[:, None, None]
    pack = jnp.concatenate([coupling.reshape(OWN, CH), thresholds[:, None], jnp.zeros((OWN, 128 - CH - 1), F32)], axis=1)
    surface_all = jnp.pad(surface.reshape(OWN, 128), ((0, 256 - OWN), (0, 0)))
    strip = jnp.swapaxes(outer_state[:, :, :PTS], 1, 2).reshape(2 * PTS, OWN)
    strip = jnp.pad(strip, ((0, 0), (0, 256 - OWN)))
    strip_levels = jnp.pad(thresholds[None, :], ((0, 0), (0, 256 - OWN)))

    edges = (pltpu.VMEM((64, 128), F32), pltpu.VMEM((64, 128), F32))
    c, q, to_a, to_b = call(
        first_kernel, [sds(8, 128), sds(16, 24, 128), sds(EDGE, 128), sds(EDGE, 128)], scratch=edges
    )(where, inner_state.reshape(8, 128), live, strip, dipole, surface_all, pack)

    fs = ghost = cs = None
    window = total = None
    low_pack = high_pack = None
    for index in range(STEPS * ORDER):
        step, power = index // ORDER, index % ORDER + 1
        first = index == 0
        factor = time_step / power
        from_a = lax.ppermute(to_a, "inner", swap)
        from_b = lax.ppermute(to_b, "inner", chips)
        if first:
            q, low_pack, high_pack = call(
                functools.partial(assemble_kernel, True), [sds(16, 88, 128), sds(OWN, 128), sds(OWN, 128)]
            )(where, q, from_a, from_b, strip)
            cs = c
        else:
            q, ghost = call(functools.partial(assemble_kernel, False), [sds(16, 24, 128), sds(32, 128)])(
                where, q, from_a, from_b
            )
        arrived = lax.all_to_all(q, "outer", split_axis=0, concat_axis=0, tiled=True)

        if first:
            tail, head, _ = lax.optimization_barrier((outer_state[:, :, 384:], outer_state[:, :, :128], q[0, 0, 0]))
            is_odd = (o % 2) == 1
            by_even = lax.ppermute(jnp.where(is_odd, head, tail), "outer", even)
            by_odd = lax.ppermute(jnp.where(is_odd, tail, head), "outer", odd)
            right = jnp.where(is_odd, by_odd, by_even)
            left = jnp.where(is_odd, by_even, by_odd)
            (bulk,) = call(window_kernel, [sds(OWN, 2 * WIDTH)], smem=0)(outer_state, left, right)
            packs = jnp.concatenate([low_pack, pack, high_pack], axis=0)
            couplings = coupling_matrix(packs[:, :CH].reshape(3 * LB, CH, CH))
            own = couplings[OWN : 2 * OWN]
            pairs = jnp.concatenate(
                [own[:, OWN : 2 * OWN], own[:, 2 * OWN : 2 * OWN + CH], own[:, OWN - CH : OWN]], axis=1
            )
            pairs = jnp.pad(pairs, ((0, 256 - OWN), (0, 16)))
        phase = index % ORDER
        if phase == 0:
            sent, _ = lax.optimization_barrier((bulk, q[0, 0, 0]))
            by_swap = lax.ppermute(sent, "inner", swap)
            by_chip = lax.ppermute(sent, "inner", chips)
            is_upper = (i % 2) == 1
            window = (by_swap, by_chip, is_upper)
        elif phase == 1:
            by_swap, by_chip, is_upper = window
            low = jnp.where(is_upper, by_swap, by_chip)
            high = jnp.where(is_upper, by_chip, by_swap)
            low, high, _ = lax.optimization_barrier((low, high, q[0, 0, 0]))
            window, total = call(
                functools.partial(bulk_kernel, step, (1, 2), True),
                [sds(3 * OWN, 2 * WIDTH), sds(OWN, 2 * WIDTH)],
                smem=2,
                scratch=(pltpu.VMEM((3 * OWN, 2 * WIDTH), F32),),
            )(where, field_strength, low, bulk, high, couplings, packs)
        elif phase == 2:
            window, total, _ = lax.optimization_barrier((window, total, q[0, 0, 0]))
            (bulk,) = call(
                functools.partial(bulk_kernel, step, (3, 4), False),
                [sds(OWN, 2 * WIDTH)],
                smem=2,
                scratch=(pltpu.VMEM((3 * OWN, 2 * WIDTH), F32), pltpu.VMEM((3 * OWN, 2 * WIDTH), F32)),
            )(where, field_strength, window, total, couplings, packs)

        given = (where, field_strength, dipole, surface_all, levels, pairs, strip_levels, arrived, cs)
        if not first:
            given = given + (fs, ghost)
        if index < STEPS * ORDER - 1:
            cs, fs, q, to_a, to_b = call(
                functools.partial(middle_kernel, first, power == ORDER, factor, step),
                [sds(16, 128), sds(64, 256), sds(16, 24, 128), sds(64, 128), sds(64, 128)],
                smem=2,
                scratch=edges,
            )(*given)
        else:
            c, grid = call(functools.partial(last_kernel, factor, step), [sds(8, 128), sds(2, OWN, 512)], smem=2)(
                *given, bulk
            )
    return c.reshape(2, LB, 128), grid


def solution(mesh):
    placed = (
        P(None, "inner", "outer"),
        P(None, "inner", "outer"),
        P("inner", "outer"),
        P("inner", "outer", None),
        P("inner", None, "outer"),
        P("inner"),
        P("inner", None, None),
        P("inner", None, None),
        P("inner"),
        P(),
    )
    return jax.shard_map(
        local,
        mesh=mesh,
        in_specs=placed,
        out_specs=(P(None, "inner", "outer"), P(None, "inner", "outer")),
        check_vma=False,
    )
```

```python
import functools

import jax
import jax.numpy as jnp
from jax import lax
from jax.experimental import pallas as pl
from jax.experimental.pallas import tpu as pltpu
from jax.sharding import PartitionSpec as P

STEPS = 2
ORDER = 4
kinetic_scale = 3.125
time_step = 0.1

F32 = jnp.float32
BF16 = jnp.bfloat16
HIGHEST = lax.Precision.HIGHEST
VM = pl.BlockSpec(memory_space=pltpu.VMEM)
SM = pl.BlockSpec(memory_space=pltpu.SMEM)
HBM = pl.BlockSpec(memory_space=pltpu.HBM)
DIPOLE = (pltpu.VMEM((4, 128, 2048), jnp.float32), pltpu.SemaphoreType.DMA((4,)))

LB = 4
CH = 40
OWN = LB * CH
PTS = 16
HALO = 8
WIDTH = 640
EDGE = 64 + OWN
NT = (((1,), (1,)), ((), ()))


def sds(*shape):
    return jax.ShapeDtypeStruct(shape, F32)


def call(kernel, outs, smem=1, scratch=(), limit=20, hbm=()):
    def run(*args):
        return pl.pallas_call(
            kernel,
            out_shape=outs,
            in_specs=[SM] * smem + [HBM if n in hbm else VM for n in range(smem, len(args))],
            out_specs=[VM] * len(outs),
            scratch_shapes=list(scratch),
            compiler_params=pltpu.CompilerParams(vmem_limit_bytes=limit << 20),
        )(*args)

    return run


def rows_of(lines, shape):
    return lax.broadcasted_iota(jnp.int32, shape, lines)


def block_mask():
    lanes = rows_of(1, (8, 256))
    first = (rows_of(0, (8, 256)) % LB) * CH
    return jnp.where((lanes >= first) & (lanes < first + CH), 1.0, 0.0).astype(F32)


def edge_tiles(strip):
    lanes = rows_of(1, (2 * PTS, 128))
    up = pltpu.roll(strip, 80, 1)[:, 128:]
    down = pltpu.roll(strip, 160, 1)[:, 128:]
    zero = jnp.zeros_like(up)
    up = jnp.where((lanes >= 72) & (lanes < 112), up, zero)
    down = jnp.where((lanes >= 32) & (lanes < 72), down, zero)
    return up, down


def emit(parity, c, strip, dipole, surface, q_ref, a_ref, b_ref, up_ref, down_ref, copies=None):
    ahead = jnp.concatenate([c[1:4], c[0:1], c[5:8], c[4:5]], axis=0)
    partial = lax.dot_general(c, surface[...], NT, precision=HIGHEST, preferred_element_type=F32)
    partial = partial * block_mask()
    b_re = jnp.sum(partial[0:4], axis=0, keepdims=True)
    b_im = jnp.sum(partial[4:8], axis=0, keepdims=True)
    tail = jnp.concatenate(
        [b_re[:, :128], b_re[:, 128:], b_im[:, :128], b_im[:, 128:], jnp.zeros((4, 128), F32)], axis=0
    )
    for s in range(16):
        q_ref[s, 0:8, :] = ahead
        q_ref[s, 8:16, :] = jnp.zeros((8, 128), F32)
        q_ref[s, 16:24, :] = tail
    for l in range(LB):
        re = jnp.broadcast_to(c[l : l + 1], (128, 128)).T
        im = jnp.broadcast_to(c[4 + l : 5 + l], (128, 128)).T
        if copies is not None:
            copies[l].wait()

        def body(s, carry):
            tile = dipole[l, :, pl.ds(pl.multiple_of(s * 128, 128), 128)]
            sum_re = jnp.sum(tile * re, axis=0, keepdims=True)
            sum_im = jnp.sum(tile * im, axis=0, keepdims=True)
            if l < LB - 1:
                q_ref[s, 9 + l : 10 + l, :] = sum_re
                q_ref[s, 13 + l : 14 + l, :] = sum_im
            else:
                up_ref[pl.ds(s, 1), :] = sum_re
                up_ref[pl.ds(16 + s, 1), :] = sum_im
            return carry

        lax.fori_loop(0, 16, body, 0, unroll=16)
    up, down = edge_tiles(strip)
    up_ref[32:64, :] = up
    down_ref[0:8, :] = c
    down_ref[8:32, :] = jnp.zeros((24, 128), F32)
    down_ref[32:64, :] = down

    @pl.when(parity == 0)
    def _():
        a_ref[0:64, :] = up_ref[...]
        b_ref[0:64, :] = down_ref[...]

    @pl.when(parity != 0)
    def _():
        a_ref[0:64, :] = down_ref[...]
        b_ref[0:64, :] = up_ref[...]


def fetch(dipole, target, arrivals):
    copies = [pltpu.make_async_copy(dipole.at[l], target.at[l], arrivals.at[l]) for l in range(LB)]
    for copy in copies:
        copy.start()
    return copies


def first_kernel(
    where,
    sizes,
    inner,
    energies,
    surface,
    coef,
    pattern,
    thresholds,
    dipole,
    outer,
    cs_ref,
    fs_ref,
    q_ref,
    a_ref,
    b_ref,
    levels_ref,
    surface_ref,
    pack_ref,
    strip_levels_ref,
    up_ref,
    down_ref,
    dipole_ref,
    dipole_arrivals,
    inner_v,
    energies_v,
    surface_v,
    coef_v,
    pattern_v,
    thresholds_v,
    corner_v,
    arrivals,
):
    copies = [
        pltpu.make_async_copy(source, target, arrivals.at[n])
        for n, (source, target) in enumerate(
            [
                (inner, inner_v),
                (energies, energies_v),
                (surface, surface_v),
                (coef, coef_v),
                (pattern, pattern_v),
                (thresholds, thresholds_v),
                (outer.at[:, :, pl.ds(0, 128)], corner_v),
            ]
        )
    ]
    for copy in copies:
        copy.start()
    fetched = fetch(dipole, dipole_ref, dipole_arrivals)
    for copy in copies:
        copy.wait()
    position = where[1] * 128 + rows_of(1, (1, 128))
    for l in range(LB):
        live = jnp.where(position < sizes[l], 1.0, 0.0).astype(F32)
        levels_ref[8 + l : 9 + l, :] = live
        levels_ref[12 + l : 13 + l, :] = live
        surface_ref[l * CH : (l + 1) * CH, :] = surface_v[l]
    levels_ref[0:4, :] = energies_v[...]
    levels_ref[4:8, :] = energies_v[...]
    surface_ref[OWN:256, :] = jnp.zeros((256 - OWN, 128), F32)
    level_lane = jnp.concatenate([thresholds_v[...], jnp.zeros((1, 256 - OWN), F32)], axis=1)
    strip_levels_ref[...] = level_lane
    column = jnp.broadcast_to(level_lane, (128, 256)).T[:OWN]
    pack_ref[...] = jnp.where(rows_of(1, (OWN, 128)) == CH, column, 0.0)
    for l in range(LB):
        block = coef_v[l] * pattern_v[l].astype(F32)
        if l == LB - 1:
            block = block * jnp.where(where[2] != 0, 1.0, 0.0).astype(F32)
        pack_ref[l * CH : (l + 1) * CH, 0:CH] = block
    for part in range(2):
        corner = jnp.concatenate([corner_v[part], jnp.zeros((256 - OWN, 128), F32)], axis=0).T[:PTS]
        fs_ref[part * PTS : (part + 1) * PTS, :] = corner
    fs_ref[32:64, :] = jnp.zeros((32, 256), F32)
    c = jnp.concatenate([inner_v[0], inner_v[1]], axis=0) * levels_ref[8:16, :]
    cs_ref[0:8, :] = c
    cs_ref[8:16, :] = c
    a_ref[64:EDGE, :] = pack_ref[...]
    b_ref[64:EDGE, :] = pack_ref[...]
    emit(where[0], c, fs_ref[0:32, :], dipole_ref, surface_ref, q_ref, a_ref, b_ref, up_ref, down_ref, fetched)


def received(parity, a, b):
    flag = jnp.full(a.shape, parity, jnp.int32) == 0
    return jnp.where(flag, b, a), jnp.where(flag, a, b)


def assemble_kernel(first, where, *refs):
    if first:
        q, a, b, strip, out_ref, low_ref, high_ref, ghost_ref = refs
    else:
        q, a, b, out_ref, ghost_ref = refs
    up, down = received(where[0], a[...], b[...])
    out_ref[:, 0:24, :] = q[...]
    for s in range(16):
        out_ref[s, 3:4, :] = down[0:1]
        out_ref[s, 7:8, :] = down[4:5]
        out_ref[s, 8:9, :] = up[s : s + 1]
        out_ref[s, 12:13, :] = up[16 + s : 17 + s]
    ghost = up[32:64] + down[32:64]
    if first:
        whole = strip[0:32, :]
        near, far = whole[:, :128], whole[:, 128:] + ghost
        for s in range(16):
            for at, value in ((24, near), (40, far)):
                out_ref[s, at : at + 8, :] = value[0:8]
                out_ref[s, at + 8 : at + 16, :] = value[PTS : PTS + 8]
        ghost_ref[...] = ghost
        low_ref[...] = up[64:EDGE]
        high_ref[...] = down[64:EDGE]
    else:
        ghost_ref[...] = ghost


def advance(copies, first, last_power, factor, field, dipole, surface, levels, pairs, thresholds, arrived, cs, fs, ghost):
    sums = []
    for l in range(LB):
        if copies is not None:
            copies[l].wait()

        def body(s, carry):
            tile = dipole[l, :, pl.ds(pl.multiple_of(s * 128, 128), 128)]
            return (
                carry[0] + tile * arrived[s, l : l + 1, :],
                carry[1] + tile * arrived[s, 4 + l : 5 + l, :],
            )

        zero = jnp.zeros((128, 128), F32)
        re, im = lax.fori_loop(0, 16, body, (zero, zero), unroll=16)
        sums.append((jnp.sum(re.T, axis=0, keepdims=True), jnp.sum(im.T, axis=0, keepdims=True)))
    forward = jnp.concatenate([a for a, _ in sums] + [b for _, b in sums], axis=0)
    backward = arrived[0, 8:16, :]
    tail = arrived[0, 16:24, :]
    for s in range(1, 16):
        backward = backward + arrived[s, 8:16, :]
        tail = tail + arrived[s, 16:24, :]
    lanes = rows_of(1, (2 * PTS, 256))
    own = fs[0:32, :]
    strip_sum = fs[32:64, :]
    near, far = own[:, :128], own[:, 128:] + ghost[...]
    if first:
        near = jnp.concatenate(
            [arrived[0, 24:32, :], near[8:16], arrived[0, 32:40, :], near[PTS + 8 : PTS + 16]], axis=0
        )
        far = jnp.concatenate([arrived[0, 40:48, :], far[8:16], arrived[0, 48:56, :], far[PTS + 8 : PTS + 16]], axis=0)
    whole = jnp.concatenate([near, far], axis=1)
    if first:
        own = jnp.where(lanes < OWN, whole, 0.0)
        strip_sum = own
    c = cs[0:8, :]
    c_sum = cs[8:16, :]
    edge = jnp.concatenate(
        [jnp.broadcast_to(own[0:1], (4, 256)), jnp.broadcast_to(own[PTS : PTS + 1], (4, 256))], axis=0
    )
    surf = jnp.dot(edge * block_mask(), surface[...], precision=HIGHEST, preferred_element_type=F32)
    image = levels[8:16, :] * (levels[0:8, :] * c + field * (forward + backward) - kinetic_scale * surf)
    c_new = jnp.concatenate([factor * image[4:8], -factor * image[0:4]], axis=0)
    coupled = lax.dot_general(whole, pairs[...], NT, precision=HIGHEST, preferred_element_type=F32)
    b_re = jnp.concatenate([tail[0:1], tail[1:2]], axis=1)
    b_im = jnp.concatenate([tail[2:3], tail[3:4]], axis=1)
    points = rows_of(0, (2 * PTS, 256))
    left = pltpu.roll(own, 1, 0)
    left = jnp.where(points == 0, b_re, jnp.where(points == PTS, b_im, left))
    right = pltpu.roll(own, 2 * PTS - 1, 0)
    right = jnp.where((points == PTS - 1) | (points == 2 * PTS - 1), 0.0, right)
    grid = kinetic_scale * (2.0 * own - left - right) + thresholds[...] * own + field * coupled
    grid = jnp.where(lanes < OWN, grid, 0.0)
    f_new = jnp.concatenate([factor * grid[PTS:], -factor * grid[:PTS]], axis=0)
    c_sum = c_sum + c_new
    strip_sum = strip_sum + f_new
    if last_power:
        return c_sum, c_sum, strip_sum, strip_sum
    return c_new, c_sum, f_new, strip_sum


def middle_kernel(away, first, last_power, factor, step, where, strengths, *refs):
    dipole, surface, levels, pairs, thresholds, arrived, cs = refs[:7]
    rest = refs[7:]
    copies = None
    if away:
        copies = fetch(dipole, *rest[-2:])
        dipole, rest = rest[-2], rest[:-2]
    fs, ghost = rest[:2]
    rest = rest[2:]
    cs_ref, fs_ref, q_ref, a_ref, b_ref, up_ref, down_ref = rest
    c, c_sum, f, f_sum = advance(
        copies,
        first,
        last_power,
        factor,
        strengths[step],
        dipole,
        surface,
        levels,
        pairs,
        thresholds,
        arrived,
        cs,
        fs,
        ghost,
    )
    cs_ref[0:8, :] = c
    cs_ref[8:16, :] = c_sum
    fs_ref[0:32, :] = f
    fs_ref[32:64, :] = f_sum
    emit(where[0], c, f, dipole, surface, q_ref, a_ref, b_ref, up_ref, down_ref)


def last_kernel(away, factor, step, where, strengths, *refs):
    dipole, rest, copies = refs[0], refs[1:], None
    if away:
        copies = fetch(dipole, *rest[-2:])
        dipole, rest = rest[-2], rest[:-2]
    *given, bulk, c_ref, out_ref = rest
    _, c_sum, _, f_sum = advance(copies, False, True, factor, strengths[step], dipole, *given)
    c_ref[...] = c_sum
    lanes = rows_of(1, (OWN, 128))
    low = jnp.full((OWN, 128), where[1], jnp.int32) == 0
    fixed = (lanes < HALO) & low
    for part in range(2):
        corner = f_sum[part * PTS : (part + 1) * PTS]
        corner = jnp.concatenate([corner, jnp.zeros((128 - PTS, 256), F32)], axis=0).T[:OWN]
        base = part * WIDTH
        out_ref[part, :, 0:128] = jnp.where(fixed, corner, bulk[:, base : base + 128])
        out_ref[part, :, 128:512] = bulk[:, base + 128 : base + 512]


def window_kernel(where, outer, by_even, by_odd, out_ref):
    lanes = rows_of(1, (OWN, 128))
    flag = jnp.full((OWN, 128), where[1] % 2, jnp.int32) == 0
    for part in range(2):
        base = part * WIDTH
        right = jnp.where(flag, by_even[part], by_odd[part])
        left = jnp.where(flag, by_odd[part], by_even[part])
        out_ref[:, base : base + 512] = outer[part]
        out_ref[:, base + 512 : base + WIDTH] = jnp.where(
            lanes < HALO, right, jnp.where(lanes >= 128 - HALO, left, 0.0)
        )


def bulk_kernel(step, powers, where, strengths, *refs):
    begin, end = powers[0] == 1, powers[-1] == ORDER
    if begin:
        own, by_swap, by_chip, couplings, pack = refs[:5]
        refs = refs[5:]
    else:
        given, given_sum, couplings, pack = refs[:4]
        refs = refs[4:]
    if end:
        sum_ref, spare, other = refs
    else:
        other, sum_ref, spare = refs
    source, target = (spare, other) if len(powers) % 2 else (other, spare)
    if begin:
        source[160:320, :] = own[...]
        sum_ref[...] = own[...]

        @pl.when(where[0] == 0)
        def _():
            source[0:160, :] = by_chip[...]
            source[320:480, :] = by_swap[...]

        @pl.when(where[0] != 0)
        def _():
            source[0:160, :] = by_swap[...]
            source[320:480, :] = by_chip[...]
    else:
        source[...] = given[...]
        sum_ref[...] = given_sum[...]
    field = strengths[step]
    lanes = rows_of(1, (1, WIDTH))
    past = (lanes >= 512) & (lanes < 512 + 64) & (jnp.full((1, WIDTH), where[1], jnp.int32) == where[3])
    keep = jnp.where(past, 0.0, 1.0).astype(F32)
    for power in powers:
        factor = time_step / power
        ring = CH * power
        groups = [(160, 320, 120, 360)]
        if power < ORDER:
            groups += [(ring, 160, ring - CH, 200), (320, 480 - ring, 280, 480 - ring + CH)]
        for out0, out1, in0, in1 in groups:
            matrix = couplings[out0:out1, in0:in1]
            m_hi = matrix.astype(BF16)
            m_lo = (matrix - m_hi.astype(F32)).astype(BF16)
            images = []
            for part in range(2):
                cols = slice(part * WIDTH, (part + 1) * WIDTH)
                f = source[in0:in1, cols]
                f_hi = f.astype(BF16)
                f_lo = (f - f_hi.astype(F32)).astype(BF16)
                coupled = jnp.dot(m_hi, f_hi, preferred_element_type=F32)
                coupled = coupled + jnp.dot(m_hi, f_lo, preferred_element_type=F32)
                coupled = coupled + jnp.dot(m_lo, f_hi, preferred_element_type=F32)
                mine = source[out0:out1, cols]
                left = pltpu.roll(mine, 1, 1)
                right = pltpu.roll(mine, WIDTH - 1, 1)
                level = pack[out0:out1, CH : CH + 1]
                image = kinetic_scale * (2.0 * mine - left - right) + level * mine + field * coupled
                images.append(image * keep)
            new_re = factor * images[1]
            new_im = -factor * images[0]
            if power < ORDER:
                target[out0:out1, 0:WIDTH] = new_re
                target[out0:out1, WIDTH : 2 * WIDTH] = new_im
            if out0 == 160:
                sum_ref[:, 0:WIDTH] = sum_ref[:, 0:WIDTH] + new_re
                sum_ref[:, WIDTH : 2 * WIDTH] = sum_ref[:, WIDTH : 2 * WIDTH] + new_im
        if not end and power == powers[-1]:
            target[0:ring, :] = jnp.zeros((ring, 2 * WIDTH), F32)
            target[480 - ring : 480, :] = jnp.zeros((ring, 2 * WIDTH), F32)
        source, target = target, source


def pair_up(lower, upper):
    return [(a, b) for a, b in zip(lower, upper)] + [(b, a) for a, b in zip(lower, upper)]


def couplings_kernel(low, own, high, couplings_ref, pairs_ref, pack_ref):
    pack_ref[0:OWN, :] = low[...]
    pack_ref[OWN : 2 * OWN, :] = own[...]
    pack_ref[2 * OWN :, :] = high[...]
    couplings_ref[...] = jnp.zeros((3 * OWN, 3 * OWN), F32)
    pairs_ref[...] = jnp.zeros((256, 256), F32)
    for w in range(3 * LB - 1):
        here, there = slice(w * CH, (w + 1) * CH), slice((w + 1) * CH, (w + 2) * CH)
        block = pack_ref[here, 0:CH]
        couplings_ref[here, there] = block
        couplings_ref[there, here] = block.T
        n = w - LB
        if 0 <= n < LB:
            pairs_ref[n * CH : (n + 1) * CH, (n + 1) * CH : (n + 2) * CH] = block
        if -1 <= n < LB - 1:
            at = n * CH if n >= 0 else OWN + CH
            pairs_ref[(n + 1) * CH : (n + 2) * CH, at : at + CH] = block.T


def after(values, token):
    return lax.optimization_barrier((values, token))[0]


WINDOWS = {3: (0, (1, 2, 3, 4)), 7: (1, (1, 2, 3, 4))}
AWAY = (0, 1, 3, 4, 7)


def local(
    inner_state,
    outer_state,
    energies,
    dipole,
    surface,
    thresholds,
    coupling_coef,
    coupling_pattern,
    block_sizes,
    field_strength,
):
    inner_count = lax.axis_size("inner")
    outer_count = lax.axis_size("outer")
    i = lax.axis_index("inner")
    o = lax.axis_index("outer")
    parity = i % 2
    has_next = jnp.where(i < inner_count - 1, 1, 0)
    where = jnp.stack([parity, o, has_next, outer_count - 1]).astype(jnp.int32)
    swap = pair_up(range(0, inner_count, 2), range(1, inner_count, 2))
    chips = pair_up(range(1, inner_count - 1, 2), range(2, inner_count, 2))
    even = pair_up(range(0, outer_count, 2), range(1, outer_count, 2))
    odd = pair_up(range(1, outer_count - 1, 2), range(2, outer_count, 2))

    edges = (pltpu.VMEM((64, 128), F32), pltpu.VMEM((64, 128), F32))
    big = pltpu.VMEM((3 * OWN, 2 * WIDTH), F32)
    cs, fs, q, to_a, to_b, levels, surface_all, pack, strip_levels = pl.pallas_call(
        first_kernel,
        out_shape=[
            sds(16, 128),
            sds(64, 256),
            sds(16, 24, 128),
            sds(EDGE, 128),
            sds(EDGE, 128),
            sds(16, 128),
            sds(256, 128),
            sds(OWN, 128),
            sds(1, 256),
        ],
        in_specs=[SM, SM] + [HBM] * 8,
        out_specs=[VM] * 9,
        scratch_shapes=[
            *edges,
            *DIPOLE,
            pltpu.VMEM((2, LB, 128), F32),
            pltpu.VMEM((LB, 128), F32),
            pltpu.VMEM((LB, CH, 128), F32),
            pltpu.VMEM((LB, CH, CH), F32),
            pltpu.VMEM((LB, CH, CH), jnp.int32),
            pltpu.VMEM((1, OWN), F32),
            pltpu.VMEM((2, OWN, 128), F32),
            pltpu.SemaphoreType.DMA((7,)),
        ],
        compiler_params=pltpu.CompilerParams(vmem_limit_bytes=20 << 20),
    )(
        where,
        block_sizes,
        *(
            pltpu.with_memory_space_constraint(x, pltpu.HBM)
            for x in (
                inner_state,
                energies,
                surface,
                coupling_coef,
                coupling_pattern,
                thresholds.reshape(1, OWN),
                dipole,
                outer_state,
            )
        ),
    )

    for index in range(STEPS * ORDER):
        step, power = index // ORDER, index % ORDER + 1
        first = index == 0
        factor = time_step / power
        from_a = lax.ppermute(to_a, "inner", swap)
        from_b = lax.ppermute(to_b, "inner", chips)
        if first:
            q, low_pack, high_pack, ghost = call(
                functools.partial(assemble_kernel, True), [sds(16, 56, 128), sds(OWN, 128), sds(OWN, 128), sds(32, 128)]
            )(where, q, from_a, from_b, fs)
        else:
            q, ghost = call(functools.partial(assemble_kernel, False), [sds(16, 24, 128), sds(32, 128)])(
                where, q, from_a, from_b
            )
        arrived = lax.all_to_all(q, "outer", split_axis=0, concat_axis=0, tiled=True)
        token = q[0, 0, 0]

        if index == 0:
            low_pack, high_pack = after((low_pack, high_pack), token)
            couplings, pairs, packs = call(
                couplings_kernel, [sds(3 * OWN, 3 * OWN), sds(256, 256), sds(3 * OWN, 128)], smem=0
            )(low_pack, pack, high_pack)
            tail, head = after((outer_state[:, :, 384:], outer_state[:, :, :128]), token)
            is_odd = (o % 2) == 1
            by_even = lax.ppermute(jnp.where(is_odd, head, tail), "outer", even)
            by_odd = lax.ppermute(jnp.where(is_odd, tail, head), "outer", odd)
            by_even, by_odd, arrived = lax.optimization_barrier((by_even, by_odd, arrived))
        if index == 1:
            by_even, by_odd = after((by_even, by_odd), token)
            (bulk,) = call(window_kernel, [sds(OWN, 2 * WIDTH)])(where, outer_state, by_even, by_odd)
            bulk, arrived = lax.optimization_barrier((bulk, arrived))
        if index in WINDOWS:
            at, powers = WINDOWS[index]
            begin, end = powers[0] == 1, powers[-1] == ORDER
            given = (bulk, by_swap, by_chip) if begin else (window, total)
            given = after(given, token)
            outs = [sds(OWN, 2 * WIDTH)] if end else [sds(3 * OWN, 2 * WIDTH), sds(OWN, 2 * WIDTH)]
            result = call(
                functools.partial(bulk_kernel, at, powers), outs, smem=2, scratch=(big, big) if end else (big,)
            )(where, field_strength, *given, couplings, packs)
            if end:
                bulk, arrived = lax.optimization_barrier((result[0], arrived))
            else:
                window, total, arrived = lax.optimization_barrier((*result, arrived))
        if index in (1, 4):
            bulk = after(bulk, token)
            by_swap = lax.ppermute(bulk, "inner", swap)
            by_chip = lax.ppermute(bulk, "inner", chips)

        away = index in AWAY
        given = (where, field_strength, pltpu.with_memory_space_constraint(dipole, pltpu.HBM) if away else dipole, surface_all, levels, pairs, strip_levels, arrived, cs, fs, ghost)
        if index < STEPS * ORDER - 1:
            cs, fs, q, to_a, to_b = call(
                functools.partial(middle_kernel, away, first, power == ORDER, factor, step),
                [sds(16, 128), sds(64, 256), sds(16, 24, 128), sds(64, 128), sds(64, 128)],
                smem=2,
                scratch=edges + DIPOLE if away else edges,
                hbm=(2,) if away else (),
            )(*given)
        else:
            c, grid = call(
                functools.partial(last_kernel, away, factor, step),
                [sds(8, 128), sds(2, OWN, 512)],
                smem=2,
                scratch=DIPOLE if away else (),
                hbm=(2,) if away else (),
            )(*given, bulk)
    return c.reshape(2, LB, 128), grid


def solution(mesh):
    placed = (
        P(None, "inner", "outer"),
        P(None, "inner", "outer"),
        P("inner", "outer"),
        P("inner", "outer", None),
        P("inner", None, "outer"),
        P("inner"),
        P("inner", None, None),
        P("inner", None, None),
        P("inner"),
        P(),
    )
    return jax.shard_map(
        local,
        mesh=mesh,
        in_specs=placed,
        out_specs=(P(None, "inner", "outer"), P(None, "inner", "outer")),
        check_vma=False,
    )
```

```python
import functools

import jax
import jax.numpy as jnp
from jax import lax
from jax.experimental import pallas as pl
from jax.experimental.pallas import tpu as pltpu
from jax.sharding import PartitionSpec as P

STEPS = 2
ORDER = 4
kinetic_scale = 3.125
time_step = 0.1

F32 = jnp.float32
BF16 = jnp.bfloat16
HIGHEST = lax.Precision.HIGHEST
VM = pl.BlockSpec(memory_space=pltpu.VMEM)
SM = pl.BlockSpec(memory_space=pltpu.SMEM)
HBM = pl.BlockSpec(memory_space=pltpu.HBM)
DIPOLE = (pltpu.VMEM((4, 128, 2048), jnp.float32), pltpu.SemaphoreType.DMA((4,)))

LB = 4
CH = 40
OWN = LB * CH
PTS = 16
HALO = 8
WIDTH = 640
EDGE = 64 + OWN
NT = (((1,), (1,)), ((), ()))


def sds(*shape):
    return jax.ShapeDtypeStruct(shape, F32)


def call(kernel, outs, smem=1, scratch=(), limit=20, hbm=()):
    def run(*args):
        return pl.pallas_call(
            kernel,
            out_shape=outs,
            in_specs=[SM] * smem + [HBM if n in hbm else VM for n in range(smem, len(args))],
            out_specs=[VM] * len(outs),
            scratch_shapes=list(scratch),
            compiler_params=pltpu.CompilerParams(vmem_limit_bytes=limit << 20),
        )(*args)

    return run


def rows_of(lines, shape):
    return lax.broadcasted_iota(jnp.int32, shape, lines)


def block_mask():
    lanes = rows_of(1, (8, 256))
    first = (rows_of(0, (8, 256)) % LB) * CH
    return jnp.where((lanes >= first) & (lanes < first + CH), 1.0, 0.0).astype(F32)


def edge_tiles(strip):
    lanes = rows_of(1, (2 * PTS, 128))
    up = pltpu.roll(strip, 80, 1)[:, 128:]
    down = pltpu.roll(strip, 160, 1)[:, 128:]
    zero = jnp.zeros_like(up)
    up = jnp.where((lanes >= 72) & (lanes < 112), up, zero)
    down = jnp.where((lanes >= 32) & (lanes < 72), down, zero)
    return up, down


def emit(parity, c, strip, dipole, surface, q_ref, a_ref, b_ref, up_ref, down_ref, copies=None):
    ahead = jnp.concatenate([c[1:4], c[0:1], c[5:8], c[4:5]], axis=0)
    partial = lax.dot_general(c, surface[...], NT, precision=HIGHEST, preferred_element_type=F32)
    partial = partial * block_mask()
    b_re = jnp.sum(partial[0:4], axis=0, keepdims=True)
    b_im = jnp.sum(partial[4:8], axis=0, keepdims=True)
    tail = jnp.concatenate(
        [b_re[:, :128], b_re[:, 128:], b_im[:, :128], b_im[:, 128:], jnp.zeros((4, 128), F32)], axis=0
    )
    for s in range(16):
        q_ref[s, 0:8, :] = ahead
        q_ref[s, 8:16, :] = jnp.zeros((8, 128), F32)
        q_ref[s, 16:24, :] = tail
    for l in range(LB):
        re = jnp.broadcast_to(c[l : l + 1], (128, 128)).T
        im = jnp.broadcast_to(c[4 + l : 5 + l], (128, 128)).T
        if copies is not None:
            copies[l].wait()

        def body(s, carry):
            tile = dipole[l, :, pl.ds(pl.multiple_of(s * 128, 128), 128)]
            sum_re = jnp.sum(tile * re, axis=0, keepdims=True)
            sum_im = jnp.sum(tile * im, axis=0, keepdims=True)
            if l < LB - 1:
                q_ref[s, 9 + l : 10 + l, :] = sum_re
                q_ref[s, 13 + l : 14 + l, :] = sum_im
            else:
                up_ref[pl.ds(s, 1), :] = sum_re
                up_ref[pl.ds(16 + s, 1), :] = sum_im
            return carry

        lax.fori_loop(0, 16, body, 0, unroll=16)
    up, down = edge_tiles(strip)
    up_ref[32:64, :] = up
    down_ref[0:8, :] = c
    down_ref[8:32, :] = jnp.zeros((24, 128), F32)
    down_ref[32:64, :] = down

    @pl.when(parity == 0)
    def _():
        a_ref[0:64, :] = up_ref[...]
        b_ref[0:64, :] = down_ref[...]

    @pl.when(parity != 0)
    def _():
        a_ref[0:64, :] = down_ref[...]
        b_ref[0:64, :] = up_ref[...]


def fetch(dipole, target, arrivals):
    copies = [pltpu.make_async_copy(dipole.at[l], target.at[l], arrivals.at[l]) for l in range(LB)]
    for copy in copies:
        copy.start()
    return copies


def first_kernel(
    where,
    sizes,
    inner,
    energies,
    surface,
    coef,
    pattern,
    thresholds,
    dipole,
    outer,
    cs_ref,
    fs_ref,
    q_ref,
    a_ref,
    b_ref,
    levels_ref,
    surface_ref,
    pack_ref,
    strip_levels_ref,
    up_ref,
    down_ref,
    dipole_ref,
    dipole_arrivals,
    inner_v,
    energies_v,
    surface_v,
    coef_v,
    pattern_v,
    thresholds_v,
    corner_v,
    arrivals,
):
    copies = [
        pltpu.make_async_copy(source, target, arrivals.at[n])
        for n, (source, target) in enumerate(
            [
                (inner, inner_v),
                (energies, energies_v),
                (surface, surface_v),
                (coef, coef_v),
                (pattern, pattern_v),
                (thresholds, thresholds_v),
                (outer.at[:, :, pl.ds(0, 128)], corner_v),
            ]
        )
    ]
    for copy in copies:
        copy.start()
    fetched = fetch(dipole, dipole_ref, dipole_arrivals)
    for copy in copies:
        copy.wait()
    position = where[1] * 128 + rows_of(1, (1, 128))
    for l in range(LB):
        live = jnp.where(position < sizes[l], 1.0, 0.0).astype(F32)
        levels_ref[8 + l : 9 + l, :] = live
        levels_ref[12 + l : 13 + l, :] = live
        surface_ref[l * CH : (l + 1) * CH, :] = surface_v[l]
    levels_ref[0:4, :] = energies_v[...]
    levels_ref[4:8, :] = energies_v[...]
    surface_ref[OWN:256, :] = jnp.zeros((256 - OWN, 128), F32)
    level_lane = jnp.concatenate([thresholds_v[...], jnp.zeros((1, 256 - OWN), F32)], axis=1)
    strip_levels_ref[...] = level_lane
    column = jnp.broadcast_to(level_lane, (128, 256)).T[:OWN]
    pack_ref[...] = jnp.where(rows_of(1, (OWN, 128)) == CH, column, 0.0)
    for l in range(LB):
        block = coef_v[l] * pattern_v[l].astype(F32)
        if l == LB - 1:
            block = block * jnp.where(where[2] != 0, 1.0, 0.0).astype(F32)
        pack_ref[l * CH : (l + 1) * CH, 0:CH] = block
    for part in range(2):
        corner = jnp.concatenate([corner_v[part], jnp.zeros((256 - OWN, 128), F32)], axis=0).T[:PTS]
        fs_ref[part * PTS : (part + 1) * PTS, :] = corner
    fs_ref[32:64, :] = jnp.zeros((32, 256), F32)
    c = jnp.concatenate([inner_v[0], inner_v[1]], axis=0) * levels_ref[8:16, :]
    cs_ref[0:8, :] = c
    cs_ref[8:16, :] = c
    a_ref[64:EDGE, :] = pack_ref[...]
    b_ref[64:EDGE, :] = pack_ref[...]
    emit(where[0], c, fs_ref[0:32, :], dipole_ref, surface_ref, q_ref, a_ref, b_ref, up_ref, down_ref, fetched)


def received(parity, a, b):
    flag = jnp.full(a.shape, parity, jnp.int32) == 0
    return jnp.where(flag, b, a), jnp.where(flag, a, b)


def assemble_kernel(first, where, *refs):
    if first:
        q, a, b, strip, out_ref, low_ref, high_ref, ghost_ref = refs
    else:
        q, a, b, out_ref, ghost_ref = refs
    up, down = received(where[0], a[...], b[...])
    out_ref[:, 0:24, :] = q[...]
    for s in range(16):
        out_ref[s, 3:4, :] = down[0:1]
        out_ref[s, 7:8, :] = down[4:5]
        out_ref[s, 8:9, :] = up[s : s + 1]
        out_ref[s, 12:13, :] = up[16 + s : 17 + s]
    ghost = up[32:64] + down[32:64]
    if first:
        whole = strip[0:32, :]
        near, far = whole[:, :128], whole[:, 128:] + ghost
        for s in range(16):
            for at, value in ((24, near), (40, far)):
                out_ref[s, at : at + 8, :] = value[0:8]
                out_ref[s, at + 8 : at + 16, :] = value[PTS : PTS + 8]
        ghost_ref[...] = ghost
        low_ref[...] = up[64:EDGE]
        high_ref[...] = down[64:EDGE]
    else:
        ghost_ref[...] = ghost


def advance(copies, first, last_power, factor, field, dipole, surface, levels, pairs, thresholds, arrived, cs, fs, ghost):
    backward = arrived[0, 8:16, :]
    tail = arrived[0, 16:24, :]
    for s in range(1, 16):
        backward = backward + arrived[s, 8:16, :]
        tail = tail + arrived[s, 16:24, :]
    lanes = rows_of(1, (2 * PTS, 256))
    own = fs[0:32, :]
    strip_sum = fs[32:64, :]
    near, far = own[:, :128], own[:, 128:] + ghost[...]
    if first:
        near = jnp.concatenate(
            [arrived[0, 24:32, :], near[8:16], arrived[0, 32:40, :], near[PTS + 8 : PTS + 16]], axis=0
        )
        far = jnp.concatenate([arrived[0, 40:48, :], far[8:16], arrived[0, 48:56, :], far[PTS + 8 : PTS + 16]], axis=0)
    whole = jnp.concatenate([near, far], axis=1)
    if first:
        own = jnp.where(lanes < OWN, whole, 0.0)
        strip_sum = own
    c = cs[0:8, :]
    c_sum = cs[8:16, :]
    edge = jnp.concatenate(
        [jnp.broadcast_to(own[0:1], (4, 256)), jnp.broadcast_to(own[PTS : PTS + 1], (4, 256))], axis=0
    )
    surf = jnp.dot(edge * block_mask(), surface[...], precision=HIGHEST, preferred_element_type=F32)
    coupled = lax.dot_general(whole, pairs[...], NT, precision=HIGHEST, preferred_element_type=F32)
    b_re = jnp.concatenate([tail[0:1], tail[1:2]], axis=1)
    b_im = jnp.concatenate([tail[2:3], tail[3:4]], axis=1)
    points = rows_of(0, (2 * PTS, 256))
    left = pltpu.roll(own, 1, 0)
    left = jnp.where(points == 0, b_re, jnp.where(points == PTS, b_im, left))
    right = pltpu.roll(own, 2 * PTS - 1, 0)
    right = jnp.where((points == PTS - 1) | (points == 2 * PTS - 1), 0.0, right)
    grid = kinetic_scale * (2.0 * own - left - right) + thresholds[...] * own + field * coupled
    grid = jnp.where(lanes < OWN, grid, 0.0)
    f_new = jnp.concatenate([factor * grid[PTS:], -factor * grid[:PTS]], axis=0)
    sums = []
    for l in range(LB):
        if copies is not None:
            copies[l].wait()

        def body(s, carry):
            tile = dipole[l, :, pl.ds(pl.multiple_of(s * 128, 128), 128)]
            return (
                carry[0] + tile * arrived[s, l : l + 1, :],
                carry[1] + tile * arrived[s, 4 + l : 5 + l, :],
            )

        zero = jnp.zeros((128, 128), F32)
        re, im = lax.fori_loop(0, 16, body, (zero, zero), unroll=16)
        sums.append((jnp.sum(re.T, axis=0, keepdims=True), jnp.sum(im.T, axis=0, keepdims=True)))
    forward = jnp.concatenate([a for a, _ in sums] + [b for _, b in sums], axis=0)
    image = levels[8:16, :] * (levels[0:8, :] * c + field * (forward + backward) - kinetic_scale * surf)
    c_new = jnp.concatenate([factor * image[4:8], -factor * image[0:4]], axis=0)
    c_sum = c_sum + c_new
    strip_sum = strip_sum + f_new
    if last_power:
        return c_sum, c_sum, strip_sum, strip_sum
    return c_new, c_sum, f_new, strip_sum


def middle_kernel(away, first, last_power, factor, step, where, strengths, *refs):
    dipole, surface, levels, pairs, thresholds, arrived, cs = refs[:7]
    rest = refs[7:]
    copies = None
    if away:
        copies = fetch(dipole, *rest[-2:])
        dipole, rest = rest[-2], rest[:-2]
    fs, ghost = rest[:2]
    rest = rest[2:]
    cs_ref, fs_ref, q_ref, a_ref, b_ref, up_ref, down_ref = rest
    c, c_sum, f, f_sum = advance(
        copies,
        first,
        last_power,
        factor,
        strengths[step],
        dipole,
        surface,
        levels,
        pairs,
        thresholds,
        arrived,
        cs,
        fs,
        ghost,
    )
    cs_ref[0:8, :] = c
    cs_ref[8:16, :] = c_sum
    fs_ref[0:32, :] = f
    fs_ref[32:64, :] = f_sum
    emit(where[0], c, f, dipole, surface, q_ref, a_ref, b_ref, up_ref, down_ref)


def last_kernel(away, factor, step, where, strengths, *refs):
    dipole, rest, copies = refs[0], refs[1:], None
    if away:
        copies = fetch(dipole, *rest[-2:])
        dipole, rest = rest[-2], rest[:-2]
    *given, bulk, c_ref, out_ref = rest
    _, c_sum, _, f_sum = advance(copies, False, True, factor, strengths[step], dipole, *given)
    c_ref[...] = c_sum
    lanes = rows_of(1, (OWN, 128))
    low = jnp.full((OWN, 128), where[1], jnp.int32) == 0
    fixed = (lanes < HALO) & low
    for part in range(2):
        corner = f_sum[part * PTS : (part + 1) * PTS]
        corner = jnp.concatenate([corner, jnp.zeros((128 - PTS, 256), F32)], axis=0).T[:OWN]
        base = part * WIDTH
        out_ref[part, :, 0:128] = jnp.where(fixed, corner, bulk[:, base : base + 128])
        out_ref[part, :, 128:512] = bulk[:, base + 128 : base + 512]


def window_kernel(where, outer, by_even, by_odd, out_ref):
    lanes = rows_of(1, (OWN, 128))
    flag = jnp.full((OWN, 128), where[1] % 2, jnp.int32) == 0
    for part in range(2):
        base = part * WIDTH
        right = jnp.where(flag, by_even[part], by_odd[part])
        left = jnp.where(flag, by_odd[part], by_even[part])
        out_ref[:, base : base + 512] = outer[part]
        out_ref[:, base + 512 : base + WIDTH] = jnp.where(
            lanes < HALO, right, jnp.where(lanes >= 128 - HALO, left, 0.0)
        )


def bulk_kernel(step, powers, where, strengths, *refs):
    begin, end = powers[0] == 1, powers[-1] == ORDER
    if begin:
        own, by_swap, by_chip, couplings, pack = refs[:5]
        refs = refs[5:]
    else:
        given, given_sum, couplings, pack = refs[:4]
        refs = refs[4:]
    if end:
        sum_ref, spare, other = refs
    else:
        other, sum_ref, spare = refs
    source, target = (spare, other) if len(powers) % 2 else (other, spare)
    if begin:
        source[160:320, :] = own[...]
        sum_ref[...] = own[...]

        @pl.when(where[0] == 0)
        def _():
            source[0:160, :] = by_chip[...]
            source[320:480, :] = by_swap[...]

        @pl.when(where[0] != 0)
        def _():
            source[0:160, :] = by_swap[...]
            source[320:480, :] = by_chip[...]
    else:
        source[...] = given[...]
        sum_ref[...] = given_sum[...]
    field = strengths[step]
    lanes = rows_of(1, (1, WIDTH - 512))
    past = (lanes < 64) & (jnp.full((1, WIDTH - 512), where[1], jnp.int32) == where[3])
    keep = jnp.where(past, 0.0, 1.0).astype(F32)
    for power in powers:
        factor = time_step / power
        ring = CH * power
        groups = [(160, 320, 120, 360)]
        if power < ORDER:
            groups += [(ring, 160, ring - CH, 200), (320, 480 - ring, 280, 480 - ring + CH)]
        for out0, out1, in0, in1 in groups:
            shape = (out1 - out0, in1 - in0)
            level = 2.0 * kinetic_scale + pack[out0:out1, CH : CH + 1]
            same = rows_of(0, shape) + out0 == rows_of(1, shape) + in0
            matrix = factor * (field * couplings[out0:out1, in0:in1] + jnp.where(same, level, 0.0))
            m_hi = matrix.astype(BF16)
            m_lo = (matrix - m_hi.astype(F32)).astype(BF16)
            images = []
            for part in range(2):
                cols = slice(part * WIDTH, (part + 1) * WIDTH)
                f = source[in0:in1, cols]
                f_hi = f.astype(BF16)
                f_lo = (f - f_hi.astype(F32)).astype(BF16)
                image = jnp.dot(m_hi, f_hi, preferred_element_type=F32)
                image = image + jnp.dot(m_hi, f_lo, preferred_element_type=F32)
                image = image + jnp.dot(m_lo, f_hi, preferred_element_type=F32)
                mine = source[out0:out1, cols]
                beside = pltpu.roll(mine, 1, 1) + pltpu.roll(mine, WIDTH - 1, 1)
                image = image - (factor * kinetic_scale) * beside
                images.append(jnp.concatenate([image[:, :512], image[:, 512:] * keep], axis=1))
            new_re = images[1]
            new_im = -images[0]
            if power < ORDER:
                target[out0:out1, 0:WIDTH] = new_re
                target[out0:out1, WIDTH : 2 * WIDTH] = new_im
            if out0 == 160:
                sum_ref[:, 0:WIDTH] = sum_ref[:, 0:WIDTH] + new_re
                sum_ref[:, WIDTH : 2 * WIDTH] = sum_ref[:, WIDTH : 2 * WIDTH] + new_im
        if not end and power == powers[-1]:
            target[0:ring, :] = jnp.zeros((ring, 2 * WIDTH), F32)
            target[480 - ring : 480, :] = jnp.zeros((ring, 2 * WIDTH), F32)
        source, target = target, source


def pair_up(lower, upper):
    return [(a, b) for a, b in zip(lower, upper)] + [(b, a) for a, b in zip(lower, upper)]


def couplings_kernel(low, own, high, couplings_ref, pairs_ref, pack_ref):
    pack_ref[0:OWN, :] = low[...]
    pack_ref[OWN : 2 * OWN, :] = own[...]
    pack_ref[2 * OWN :, :] = high[...]
    couplings_ref[...] = jnp.zeros((3 * OWN, 3 * OWN), F32)
    pairs_ref[...] = jnp.zeros((256, 256), F32)
    for w in range(3 * LB - 1):
        here, there = slice(w * CH, (w + 1) * CH), slice((w + 1) * CH, (w + 2) * CH)
        block = pack_ref[here, 0:CH]
        couplings_ref[here, there] = block
        couplings_ref[there, here] = block.T
        n = w - LB
        if 0 <= n < LB:
            pairs_ref[n * CH : (n + 1) * CH, (n + 1) * CH : (n + 2) * CH] = block
        if -1 <= n < LB - 1:
            at = n * CH if n >= 0 else OWN + CH
            pairs_ref[(n + 1) * CH : (n + 2) * CH, at : at + CH] = block.T


def after(values, token):
    return lax.optimization_barrier((values, token))[0]


WINDOWS = {3: (0, (1, 2, 3, 4)), 7: (1, (1, 2, 3, 4))}
AWAY = (0, 1, 3, 4, 7)


def local(
    inner_state,
    outer_state,
    energies,
    dipole,
    surface,
    thresholds,
    coupling_coef,
    coupling_pattern,
    block_sizes,
    field_strength,
):
    inner_count = lax.axis_size("inner")
    outer_count = lax.axis_size("outer")
    i = lax.axis_index("inner")
    o = lax.axis_index("outer")
    parity = i % 2
    has_next = jnp.where(i < inner_count - 1, 1, 0)
    where = jnp.stack([parity, o, has_next, outer_count - 1]).astype(jnp.int32)
    swap = pair_up(range(0, inner_count, 2), range(1, inner_count, 2))
    chips = pair_up(range(1, inner_count - 1, 2), range(2, inner_count, 2))
    even = pair_up(range(0, outer_count, 2), range(1, outer_count, 2))
    odd = pair_up(range(1, outer_count - 1, 2), range(2, outer_count, 2))

    edges = (pltpu.VMEM((64, 128), F32), pltpu.VMEM((64, 128), F32))
    big = pltpu.VMEM((3 * OWN, 2 * WIDTH), F32)
    cs, fs, q, to_a, to_b, levels, surface_all, pack, strip_levels = pl.pallas_call(
        first_kernel,
        out_shape=[
            sds(16, 128),
            sds(64, 256),
            sds(16, 24, 128),
            sds(EDGE, 128),
            sds(EDGE, 128),
            sds(16, 128),
            sds(256, 128),
            sds(OWN, 128),
            sds(1, 256),
        ],
        in_specs=[SM, SM] + [HBM] * 8,
        out_specs=[VM] * 9,
        scratch_shapes=[
            *edges,
            *DIPOLE,
            pltpu.VMEM((2, LB, 128), F32),
            pltpu.VMEM((LB, 128), F32),
            pltpu.VMEM((LB, CH, 128), F32),
            pltpu.VMEM((LB, CH, CH), F32),
            pltpu.VMEM((LB, CH, CH), jnp.int32),
            pltpu.VMEM((1, OWN), F32),
            pltpu.VMEM((2, OWN, 128), F32),
            pltpu.SemaphoreType.DMA((7,)),
        ],
        compiler_params=pltpu.CompilerParams(vmem_limit_bytes=20 << 20),
    )(
        where,
        block_sizes,
        *(
            pltpu.with_memory_space_constraint(x, pltpu.HBM)
            for x in (
                inner_state,
                energies,
                surface,
                coupling_coef,
                coupling_pattern,
                thresholds.reshape(1, OWN),
                dipole,
                outer_state,
            )
        ),
    )

    for index in range(STEPS * ORDER):
        step, power = index // ORDER, index % ORDER + 1
        first = index == 0
        factor = time_step / power
        from_a = lax.ppermute(to_a, "inner", swap)
        from_b = lax.ppermute(to_b, "inner", chips)
        if first:
            q, low_pack, high_pack, ghost = call(
                functools.partial(assemble_kernel, True), [sds(16, 56, 128), sds(OWN, 128), sds(OWN, 128), sds(32, 128)]
            )(where, q, from_a, from_b, fs)
        else:
            q, ghost = call(functools.partial(assemble_kernel, False), [sds(16, 24, 128), sds(32, 128)])(
                where, q, from_a, from_b
            )
        arrived = lax.all_to_all(q, "outer", split_axis=0, concat_axis=0, tiled=True)
        token = q[0, 0, 0]

        if index == 0:
            low_pack, high_pack = after((low_pack, high_pack), token)
            couplings, pairs, packs = call(
                couplings_kernel, [sds(3 * OWN, 3 * OWN), sds(256, 256), sds(3 * OWN, 128)], smem=0
            )(low_pack, pack, high_pack)
            tail, head = after((outer_state[:, :, 384:], outer_state[:, :, :128]), token)
            is_odd = (o % 2) == 1
            by_even = lax.ppermute(jnp.where(is_odd, head, tail), "outer", even)
            by_odd = lax.ppermute(jnp.where(is_odd, tail, head), "outer", odd)
            by_even, by_odd, arrived = lax.optimization_barrier((by_even, by_odd, arrived))
        if index == 1:
            by_even, by_odd = after((by_even, by_odd), token)
            (bulk,) = call(window_kernel, [sds(OWN, 2 * WIDTH)])(where, outer_state, by_even, by_odd)
            bulk, arrived = lax.optimization_barrier((bulk, arrived))
        if index in WINDOWS:
            at, powers = WINDOWS[index]
            begin, end = powers[0] == 1, powers[-1] == ORDER
            given = (bulk, by_swap, by_chip) if begin else (window, total)
            given = after(given, token)
            outs = [sds(OWN, 2 * WIDTH)] if end else [sds(3 * OWN, 2 * WIDTH), sds(OWN, 2 * WIDTH)]
            result = call(
                functools.partial(bulk_kernel, at, powers), outs, smem=2, scratch=(big, big) if end else (big,)
            )(where, field_strength, *given, couplings, packs)
            if end:
                bulk, arrived = lax.optimization_barrier((result[0], arrived))
            else:
                window, total, arrived = lax.optimization_barrier((*result, arrived))
        if index in (1, 4):
            bulk = after(bulk, token)
            by_swap = lax.ppermute(bulk, "inner", swap)
            by_chip = lax.ppermute(bulk, "inner", chips)

        away = index in AWAY
        given = (where, field_strength, pltpu.with_memory_space_constraint(dipole, pltpu.HBM) if away else dipole, surface_all, levels, pairs, strip_levels, arrived, cs, fs, ghost)
        if index < STEPS * ORDER - 1:
            cs, fs, q, to_a, to_b = call(
                functools.partial(middle_kernel, away, first, power == ORDER, factor, step),
                [sds(16, 128), sds(64, 256), sds(16, 24, 128), sds(64, 128), sds(64, 128)],
                smem=2,
                scratch=edges + DIPOLE if away else edges,
                hbm=(2,) if away else (),
            )(*given)
        else:
            c, grid = call(
                functools.partial(last_kernel, away, factor, step),
                [sds(8, 128), sds(2, OWN, 512)],
                smem=2,
                scratch=DIPOLE if away else (),
                hbm=(2,) if away else (),
            )(*given, bulk)
    return c.reshape(2, LB, 128), grid


def solution(mesh):
    placed = (
        P(None, "inner", "outer"),
        P(None, "inner", "outer"),
        P("inner", "outer"),
        P("inner", "outer", None),
        P("inner", None, "outer"),
        P("inner"),
        P("inner", None, None),
        P("inner", None, None),
        P("inner"),
        P(),
    )
    return jax.shard_map(
        local,
        mesh=mesh,
        in_specs=placed,
        out_specs=(P(None, "inner", "outer"), P(None, "inner", "outer")),
        check_vma=False,
    )
```

```python
import functools

import jax
import jax.numpy as jnp
from jax import lax
from jax.experimental import pallas as pl
from jax.experimental.pallas import tpu as pltpu
from jax.sharding import PartitionSpec as P

STEPS = 2
ORDER = 4
kinetic_scale = 3.125
time_step = 0.1

F32 = jnp.float32
BF16 = jnp.bfloat16
HIGHEST = lax.Precision.HIGHEST
VM = pl.BlockSpec(memory_space=pltpu.VMEM)
SM = pl.BlockSpec(memory_space=pltpu.SMEM)
HBM = pl.BlockSpec(memory_space=pltpu.HBM)
DIPOLE = (pltpu.VMEM((4, 128, 2048), jnp.float32), pltpu.SemaphoreType.DMA((4,)))

LB = 4
CH = 40
OWN = LB * CH
PTS = 16
HALO = 8
WIDTH = 640
EDGE = 64 + OWN
NT = (((1,), (1,)), ((), ()))


def sds(*shape):
    return jax.ShapeDtypeStruct(shape, F32)


def call(kernel, outs, smem=1, scratch=(), limit=20, hbm=()):
    def run(*args):
        return pl.pallas_call(
            kernel,
            out_shape=outs,
            in_specs=[SM] * smem + [HBM if n in hbm else VM for n in range(smem, len(args))],
            out_specs=[VM] * len(outs),
            scratch_shapes=list(scratch),
            compiler_params=pltpu.CompilerParams(vmem_limit_bytes=limit << 20),
        )(*args)

    return run


def rows_of(lines, shape):
    return lax.broadcasted_iota(jnp.int32, shape, lines)


def block_mask():
    lanes = rows_of(1, (8, 256))
    first = (rows_of(0, (8, 256)) % LB) * CH
    return jnp.where((lanes >= first) & (lanes < first + CH), 1.0, 0.0).astype(F32)


def edge_tiles(strip):
    lanes = rows_of(1, (2 * PTS, 128))
    up = pltpu.roll(strip, 80, 1)[:, 128:]
    down = pltpu.roll(strip, 160, 1)[:, 128:]
    zero = jnp.zeros_like(up)
    up = jnp.where((lanes >= 72) & (lanes < 112), up, zero)
    down = jnp.where((lanes >= 32) & (lanes < 72), down, zero)
    return up, down


def emit(parity, c, strip, dipole, surface, q_ref, a_ref, b_ref, up_ref, down_ref, copies=None):
    ahead = jnp.concatenate([c[1:4], c[0:1], c[5:8], c[4:5]], axis=0)
    partial = lax.dot_general(c, surface[...], NT, precision=HIGHEST, preferred_element_type=F32)
    partial = partial * block_mask()
    b_re = jnp.sum(partial[0:4], axis=0, keepdims=True)
    b_im = jnp.sum(partial[4:8], axis=0, keepdims=True)
    tail = jnp.concatenate(
        [b_re[:, :128], b_re[:, 128:], b_im[:, :128], b_im[:, 128:], jnp.zeros((4, 128), F32)], axis=0
    )
    for s in range(16):
        q_ref[s, 0:8, :] = ahead
        q_ref[s, 8:16, :] = jnp.zeros((8, 128), F32)
        q_ref[s, 16:24, :] = tail
    for l in range(LB):
        re = jnp.broadcast_to(c[l : l + 1], (128, 128)).T
        im = jnp.broadcast_to(c[4 + l : 5 + l], (128, 128)).T
        if copies is not None:
            copies[l].wait()

        def body(s, carry):
            tile = dipole[l, :, pl.ds(pl.multiple_of(s * 128, 128), 128)]
            sum_re = jnp.sum(tile * re, axis=0, keepdims=True)
            sum_im = jnp.sum(tile * im, axis=0, keepdims=True)
            if l < LB - 1:
                q_ref[s, 9 + l : 10 + l, :] = sum_re
                q_ref[s, 13 + l : 14 + l, :] = sum_im
            else:
                up_ref[pl.ds(s, 1), :] = sum_re
                up_ref[pl.ds(16 + s, 1), :] = sum_im
            return carry

        lax.fori_loop(0, 16, body, 0, unroll=16)
    up, down = edge_tiles(strip)
    up_ref[32:64, :] = up
    down_ref[0:8, :] = c
    down_ref[8:32, :] = jnp.zeros((24, 128), F32)
    down_ref[32:64, :] = down

    @pl.when(parity == 0)
    def _():
        a_ref[0:64, :] = up_ref[...]
        b_ref[0:64, :] = down_ref[...]

    @pl.when(parity != 0)
    def _():
        a_ref[0:64, :] = down_ref[...]
        b_ref[0:64, :] = up_ref[...]


def fetch(dipole, target, arrivals):
    copies = [pltpu.make_async_copy(dipole.at[l], target.at[l], arrivals.at[l]) for l in range(LB)]
    for copy in copies:
        copy.start()
    return copies


def first_kernel(
    where,
    sizes,
    inner,
    energies,
    surface,
    coef,
    pattern,
    thresholds,
    dipole,
    outer,
    cs_ref,
    fs_ref,
    q_ref,
    a_ref,
    b_ref,
    levels_ref,
    surface_ref,
    pack_ref,
    strip_levels_ref,
    up_ref,
    down_ref,
    dipole_ref,
    dipole_arrivals,
    inner_v,
    energies_v,
    surface_v,
    coef_v,
    pattern_v,
    thresholds_v,
    corner_v,
    arrivals,
):
    copies = [
        pltpu.make_async_copy(source, target, arrivals.at[n])
        for n, (source, target) in enumerate(
            [
                (inner, inner_v),
                (energies, energies_v),
                (surface, surface_v),
                (coef, coef_v),
                (pattern, pattern_v),
                (thresholds, thresholds_v),
                (outer.at[:, :, pl.ds(0, 128)], corner_v),
            ]
        )
    ]
    for copy in copies:
        copy.start()
    fetched = fetch(dipole, dipole_ref, dipole_arrivals)
    for copy in copies:
        copy.wait()
    position = where[1] * 128 + rows_of(1, (1, 128))
    for l in range(LB):
        live = jnp.where(position < sizes[l], 1.0, 0.0).astype(F32)
        levels_ref[8 + l : 9 + l, :] = live
        levels_ref[12 + l : 13 + l, :] = live
        surface_ref[l * CH : (l + 1) * CH, :] = surface_v[l]
    levels_ref[0:4, :] = energies_v[...]
    levels_ref[4:8, :] = energies_v[...]
    surface_ref[OWN:256, :] = jnp.zeros((256 - OWN, 128), F32)
    level_lane = jnp.concatenate([thresholds_v[...], jnp.zeros((1, 256 - OWN), F32)], axis=1)
    strip_levels_ref[...] = level_lane
    column = jnp.broadcast_to(level_lane, (128, 256)).T[:OWN]
    pack_ref[...] = jnp.where(rows_of(1, (OWN, 128)) == CH, column, 0.0)
    for l in range(LB):
        block = coef_v[l] * pattern_v[l].astype(F32)
        if l == LB - 1:
            block = block * jnp.where(where[2] != 0, 1.0, 0.0).astype(F32)
        pack_ref[l * CH : (l + 1) * CH, 0:CH] = block
    for part in range(2):
        corner = jnp.concatenate([corner_v[part], jnp.zeros((256 - OWN, 128), F32)], axis=0).T[:PTS]
        fs_ref[part * PTS : (part + 1) * PTS, :] = corner
    fs_ref[32:64, :] = jnp.zeros((32, 256), F32)
    c = jnp.concatenate([inner_v[0], inner_v[1]], axis=0) * levels_ref[8:16, :]
    cs_ref[0:8, :] = c
    cs_ref[8:16, :] = c
    a_ref[64:EDGE, :] = pack_ref[...]
    b_ref[64:EDGE, :] = pack_ref[...]
    emit(where[0], c, fs_ref[0:32, :], dipole_ref, surface_ref, q_ref, a_ref, b_ref, up_ref, down_ref, fetched)


def received(parity, a, b):
    flag = jnp.full(a.shape, parity, jnp.int32) == 0
    return jnp.where(flag, b, a), jnp.where(flag, a, b)


def assemble_kernel(first, where, *refs):
    if first:
        q, a, b, strip, out_ref, low_ref, high_ref, ghost_ref = refs
    else:
        q, a, b, out_ref, ghost_ref = refs
    up, down = received(where[0], a[...], b[...])
    out_ref[:, 0:24, :] = q[...]
    for s in range(16):
        out_ref[s, 3:4, :] = down[0:1]
        out_ref[s, 7:8, :] = down[4:5]
        out_ref[s, 8:9, :] = up[s : s + 1]
        out_ref[s, 12:13, :] = up[16 + s : 17 + s]
    ghost = up[32:64] + down[32:64]
    if first:
        whole = strip[0:32, :]
        near, far = whole[:, :128], whole[:, 128:] + ghost
        for s in range(16):
            for at, value in ((24, near), (40, far)):
                out_ref[s, at : at + 8, :] = value[0:8]
                out_ref[s, at + 8 : at + 16, :] = value[PTS : PTS + 8]
        ghost_ref[...] = ghost
        low_ref[...] = up[64:EDGE]
        high_ref[...] = down[64:EDGE]
    else:
        ghost_ref[...] = ghost


def advance(copies, first, last_power, factor, field, dipole, surface, levels, pairs, thresholds, arrived, cs, fs, ghost):
    backward = arrived[0, 8:16, :]
    tail = arrived[0, 16:24, :]
    for s in range(1, 16):
        backward = backward + arrived[s, 8:16, :]
        tail = tail + arrived[s, 16:24, :]
    lanes = rows_of(1, (2 * PTS, 256))
    own = fs[0:32, :]
    strip_sum = fs[32:64, :]
    near, far = own[:, :128], own[:, 128:] + ghost[...]
    if first:
        near = jnp.concatenate(
            [arrived[0, 24:32, :], near[8:16], arrived[0, 32:40, :], near[PTS + 8 : PTS + 16]], axis=0
        )
        far = jnp.concatenate([arrived[0, 40:48, :], far[8:16], arrived[0, 48:56, :], far[PTS + 8 : PTS + 16]], axis=0)
    whole = jnp.concatenate([near, far], axis=1)
    if first:
        own = jnp.where(lanes < OWN, whole, 0.0)
        strip_sum = own
    c = cs[0:8, :]
    c_sum = cs[8:16, :]
    edge = jnp.concatenate(
        [jnp.broadcast_to(own[0:1], (4, 256)), jnp.broadcast_to(own[PTS : PTS + 1], (4, 256))], axis=0
    )
    surf = jnp.dot(edge * block_mask(), surface[...], precision=HIGHEST, preferred_element_type=F32)
    coupled = lax.dot_general(whole, pairs[...], NT, precision=HIGHEST, preferred_element_type=F32)
    b_re = jnp.concatenate([tail[0:1], tail[1:2]], axis=1)
    b_im = jnp.concatenate([tail[2:3], tail[3:4]], axis=1)
    points = rows_of(0, (2 * PTS, 256))
    left = pltpu.roll(own, 1, 0)
    left = jnp.where(points == 0, b_re, jnp.where(points == PTS, b_im, left))
    right = pltpu.roll(own, 2 * PTS - 1, 0)
    right = jnp.where((points == PTS - 1) | (points == 2 * PTS - 1), 0.0, right)
    grid = kinetic_scale * (2.0 * own - left - right) + thresholds[...] * own + field * coupled
    grid = jnp.where(lanes < OWN, grid, 0.0)
    f_new = jnp.concatenate([factor * grid[PTS:], -factor * grid[:PTS]], axis=0)
    sums = []
    for l in range(LB):
        if copies is not None:
            copies[l].wait()

        def body(s, carry):
            tile = dipole[l, :, pl.ds(pl.multiple_of(s * 128, 128), 128)]
            return (
                carry[0] + tile * arrived[s, l : l + 1, :],
                carry[1] + tile * arrived[s, 4 + l : 5 + l, :],
            )

        zero = jnp.zeros((128, 128), F32)
        re, im = lax.fori_loop(0, 16, body, (zero, zero), unroll=16)
        sums.append((jnp.sum(re.T, axis=0, keepdims=True), jnp.sum(im.T, axis=0, keepdims=True)))
    forward = jnp.concatenate([a for a, _ in sums] + [b for _, b in sums], axis=0)
    image = levels[8:16, :] * (levels[0:8, :] * c + field * (forward + backward) - kinetic_scale * surf)
    c_new = jnp.concatenate([factor * image[4:8], -factor * image[0:4]], axis=0)
    c_sum = c_sum + c_new
    strip_sum = strip_sum + f_new
    if last_power:
        return c_sum, c_sum, strip_sum, strip_sum
    return c_new, c_sum, f_new, strip_sum


def middle_kernel(away, first, last_power, factor, step, where, strengths, *refs):
    dipole, surface, levels, pairs, thresholds, arrived, cs = refs[:7]
    rest = refs[7:]
    copies = None
    if away:
        copies = fetch(dipole, *rest[-2:])
        dipole, rest = rest[-2], rest[:-2]
    fs, ghost = rest[:2]
    rest = rest[2:]
    cs_ref, fs_ref, q_ref, a_ref, b_ref, up_ref, down_ref = rest
    c, c_sum, f, f_sum = advance(
        copies,
        first,
        last_power,
        factor,
        strengths[step],
        dipole,
        surface,
        levels,
        pairs,
        thresholds,
        arrived,
        cs,
        fs,
        ghost,
    )
    cs_ref[0:8, :] = c
    cs_ref[8:16, :] = c_sum
    fs_ref[0:32, :] = f
    fs_ref[32:64, :] = f_sum
    emit(where[0], c, f, dipole, surface, q_ref, a_ref, b_ref, up_ref, down_ref)


def last_kernel(factor, step, where, strengths, *refs):
    *rest, dipole_ref, dipole_arrivals, bulk_arrivals = refs
    dipole, *given, bulk, c_ref, out_ref = rest
    copies = fetch(dipole, dipole_ref, dipole_arrivals)
    moves = [
        pltpu.make_async_copy(bulk.at[:, pl.ds(part * WIDTH, 512)], out_ref.at[part], bulk_arrivals.at[part])
        for part in range(2)
    ]
    for move in moves:
        move.start()
    _, c_sum, _, f_sum = advance(copies, False, True, factor, strengths[step], dipole_ref, *given)
    c_ref[...] = c_sum
    lanes = rows_of(1, (OWN, 128))
    low = jnp.full((OWN, 128), where[1], jnp.int32) == 0
    fixed = (lanes < HALO) & low
    for part in range(2):
        corner = f_sum[part * PTS : (part + 1) * PTS]
        corner = jnp.concatenate([corner, jnp.zeros((128 - PTS, 256), F32)], axis=0).T[:OWN]
        moves[part].wait()
        out_ref[part, :, 0:128] = jnp.where(fixed, corner, out_ref[part, :, 0:128])


def window_kernel(where, outer, by_even, by_odd, out_ref):
    lanes = rows_of(1, (OWN, 128))
    flag = jnp.full((OWN, 128), where[1] % 2, jnp.int32) == 0
    for part in range(2):
        base = part * WIDTH
        right = jnp.where(flag, by_even[part], by_odd[part])
        left = jnp.where(flag, by_odd[part], by_even[part])
        out_ref[:, base : base + 512] = outer[part]
        out_ref[:, base + 512 : base + WIDTH] = jnp.where(
            lanes < HALO, right, jnp.where(lanes >= 128 - HALO, left, 0.0)
        )


def bulk_kernel(step, powers, where, strengths, *refs):
    begin, end = powers[0] == 1, powers[-1] == ORDER
    if begin:
        own, by_swap, by_chip, couplings, pack = refs[:5]
        refs = refs[5:]
    else:
        given, given_sum, couplings, pack = refs[:4]
        refs = refs[4:]
    if end:
        sum_ref, spare, other = refs
    else:
        other, sum_ref, spare = refs
    source, target = (spare, other) if len(powers) % 2 else (other, spare)
    if begin:
        source[160:320, :] = own[...]
        sum_ref[...] = own[...]

        @pl.when(where[0] == 0)
        def _():
            source[0:160, :] = by_chip[...]
            source[320:480, :] = by_swap[...]

        @pl.when(where[0] != 0)
        def _():
            source[0:160, :] = by_swap[...]
            source[320:480, :] = by_chip[...]
    else:
        source[...] = given[...]
        sum_ref[...] = given_sum[...]
    field = strengths[step]
    lanes = rows_of(1, (1, WIDTH - 512))
    past = (lanes < 64) & (jnp.full((1, WIDTH - 512), where[1], jnp.int32) == where[3])
    keep = jnp.where(past, 0.0, 1.0).astype(F32)
    for power in powers:
        factor = time_step / power
        ring = CH * power
        groups = [(160, 320, 120, 360)]
        if power < ORDER:
            groups += [(ring, 160, ring - CH, 200), (320, 480 - ring, 280, 480 - ring + CH)]
        for out0, out1, in0, in1 in groups:
            shape = (out1 - out0, in1 - in0)
            level = 2.0 * kinetic_scale + pack[out0:out1, CH : CH + 1]
            same = rows_of(0, shape) + out0 == rows_of(1, shape) + in0
            matrix = factor * (field * couplings[out0:out1, in0:in1] + jnp.where(same, level, 0.0))
            m_hi = matrix.astype(BF16)
            m_lo = (matrix - m_hi.astype(F32)).astype(BF16)
            images = []
            for part in range(2):
                cols = slice(part * WIDTH, (part + 1) * WIDTH)
                f = source[in0:in1, cols]
                f_hi = f.astype(BF16)
                f_lo = (f - f_hi.astype(F32)).astype(BF16)
                image = jnp.dot(m_hi, f_hi, preferred_element_type=F32)
                image = image + jnp.dot(m_hi, f_lo, preferred_element_type=F32)
                image = image + jnp.dot(m_lo, f_hi, preferred_element_type=F32)
                mine = source[out0:out1, cols]
                beside = pltpu.roll(mine, 1, 1) + pltpu.roll(mine, WIDTH - 1, 1)
                image = image - (factor * kinetic_scale) * beside
                images.append(jnp.concatenate([image[:, :512], image[:, 512:] * keep], axis=1))
            new_re = images[1]
            new_im = -images[0]
            if power < ORDER:
                target[out0:out1, 0:WIDTH] = new_re
                target[out0:out1, WIDTH : 2 * WIDTH] = new_im
            if out0 == 160:
                sum_ref[:, 0:WIDTH] = sum_ref[:, 0:WIDTH] + new_re
                sum_ref[:, WIDTH : 2 * WIDTH] = sum_ref[:, WIDTH : 2 * WIDTH] + new_im
        if not end and power == powers[-1]:
            target[0:ring, :] = jnp.zeros((ring, 2 * WIDTH), F32)
            target[480 - ring : 480, :] = jnp.zeros((ring, 2 * WIDTH), F32)
        source, target = target, source


def pair_up(lower, upper):
    return [(a, b) for a, b in zip(lower, upper)] + [(b, a) for a, b in zip(lower, upper)]


def couplings_kernel(low, own, high, couplings_ref, pairs_ref, pack_ref):
    pack_ref[0:OWN, :] = low[...]
    pack_ref[OWN : 2 * OWN, :] = own[...]
    pack_ref[2 * OWN :, :] = high[...]
    couplings_ref[...] = jnp.zeros((3 * OWN, 3 * OWN), F32)
    pairs_ref[...] = jnp.zeros((256, 256), F32)
    for w in range(3 * LB - 1):
        here, there = slice(w * CH, (w + 1) * CH), slice((w + 1) * CH, (w + 2) * CH)
        block = pack_ref[here, 0:CH]
        couplings_ref[here, there] = block
        couplings_ref[there, here] = block.T
        n = w - LB
        if 0 <= n < LB:
            pairs_ref[n * CH : (n + 1) * CH, (n + 1) * CH : (n + 2) * CH] = block
        if -1 <= n < LB - 1:
            at = n * CH if n >= 0 else OWN + CH
            pairs_ref[(n + 1) * CH : (n + 2) * CH, at : at + CH] = block.T


def after(values, token):
    return lax.optimization_barrier((values, token))[0]


WINDOWS = {3: (0, (1, 2, 3, 4)), 7: (1, (1, 2, 3, 4))}
AWAY = (0, 1, 3, 4, 7)


def local(
    inner_state,
    outer_state,
    energies,
    dipole,
    surface,
    thresholds,
    coupling_coef,
    coupling_pattern,
    block_sizes,
    field_strength,
):
    inner_count = lax.axis_size("inner")
    outer_count = lax.axis_size("outer")
    i = lax.axis_index("inner")
    o = lax.axis_index("outer")
    parity = i % 2
    has_next = jnp.where(i < inner_count - 1, 1, 0)
    where = jnp.stack([parity, o, has_next, outer_count - 1]).astype(jnp.int32)
    swap = pair_up(range(0, inner_count, 2), range(1, inner_count, 2))
    chips = pair_up(range(1, inner_count - 1, 2), range(2, inner_count, 2))
    even = pair_up(range(0, outer_count, 2), range(1, outer_count, 2))
    odd = pair_up(range(1, outer_count - 1, 2), range(2, outer_count, 2))

    edges = (pltpu.VMEM((64, 128), F32), pltpu.VMEM((64, 128), F32))
    big = pltpu.VMEM((3 * OWN, 2 * WIDTH), F32)
    cs, fs, q, to_a, to_b, levels, surface_all, pack, strip_levels = pl.pallas_call(
        first_kernel,
        out_shape=[
            sds(16, 128),
            sds(64, 256),
            sds(16, 24, 128),
            sds(EDGE, 128),
            sds(EDGE, 128),
            sds(16, 128),
            sds(256, 128),
            sds(OWN, 128),
            sds(1, 256),
        ],
        in_specs=[SM, SM] + [HBM] * 8,
        out_specs=[VM] * 9,
        scratch_shapes=[
            *edges,
            *DIPOLE,
            pltpu.VMEM((2, LB, 128), F32),
            pltpu.VMEM((LB, 128), F32),
            pltpu.VMEM((LB, CH, 128), F32),
            pltpu.VMEM((LB, CH, CH), F32),
            pltpu.VMEM((LB, CH, CH), jnp.int32),
            pltpu.VMEM((1, OWN), F32),
            pltpu.VMEM((2, OWN, 128), F32),
            pltpu.SemaphoreType.DMA((7,)),
        ],
        compiler_params=pltpu.CompilerParams(vmem_limit_bytes=20 << 20),
    )(
        where,
        block_sizes,
        *(
            pltpu.with_memory_space_constraint(x, pltpu.HBM)
            for x in (
                inner_state,
                energies,
                surface,
                coupling_coef,
                coupling_pattern,
                thresholds.reshape(1, OWN),
                dipole,
                outer_state,
            )
        ),
    )

    for index in range(STEPS * ORDER):
        step, power = index // ORDER, index % ORDER + 1
        first = index == 0
        factor = time_step / power
        from_a = lax.ppermute(to_a, "inner", swap)
        from_b = lax.ppermute(to_b, "inner", chips)
        if first:
            q, low_pack, high_pack, ghost = call(
                functools.partial(assemble_kernel, True), [sds(16, 56, 128), sds(OWN, 128), sds(OWN, 128), sds(32, 128)]
            )(where, q, from_a, from_b, fs)
        else:
            q, ghost = call(functools.partial(assemble_kernel, False), [sds(16, 24, 128), sds(32, 128)])(
                where, q, from_a, from_b
            )
        arrived = lax.all_to_all(q, "outer", split_axis=0, concat_axis=0, tiled=True)
        token = q[0, 0, 0]

        if index == 0:
            low_pack, high_pack = after((low_pack, high_pack), token)
            couplings, pairs, packs = call(
                couplings_kernel, [sds(3 * OWN, 3 * OWN), sds(256, 256), sds(3 * OWN, 128)], smem=0
            )(low_pack, pack, high_pack)
            tail, head = after((outer_state[:, :, 384:], outer_state[:, :, :128]), token)
            is_odd = (o % 2) == 1
            by_even = lax.ppermute(jnp.where(is_odd, head, tail), "outer", even)
            by_odd = lax.ppermute(jnp.where(is_odd, tail, head), "outer", odd)
            by_even, by_odd, arrived = lax.optimization_barrier((by_even, by_odd, arrived))
        if index == 1:
            by_even, by_odd = after((by_even, by_odd), token)
            (bulk,) = call(window_kernel, [sds(OWN, 2 * WIDTH)])(where, outer_state, by_even, by_odd)
            bulk, arrived = lax.optimization_barrier((bulk, arrived))
        if index in WINDOWS:
            at, powers = WINDOWS[index]
            begin, end = powers[0] == 1, powers[-1] == ORDER
            given = (bulk, by_swap, by_chip) if begin else (window, total)
            given = after(given, token)
            outs = [sds(OWN, 2 * WIDTH)] if end else [sds(3 * OWN, 2 * WIDTH), sds(OWN, 2 * WIDTH)]
            result = call(
                functools.partial(bulk_kernel, at, powers), outs, smem=2, scratch=(big, big) if end else (big,)
            )(where, field_strength, *given, couplings, packs)
            if end:
                bulk, arrived = lax.optimization_barrier((result[0], arrived))
            else:
                window, total, arrived = lax.optimization_barrier((*result, arrived))
        if index in (1, 4):
            bulk = after(bulk, token)
            by_swap = lax.ppermute(bulk, "inner", swap)
            by_chip = lax.ppermute(bulk, "inner", chips)

        away = index in AWAY
        given = (where, field_strength, pltpu.with_memory_space_constraint(dipole, pltpu.HBM) if away else dipole, surface_all, levels, pairs, strip_levels, arrived, cs, fs, ghost)
        if index < STEPS * ORDER - 1:
            cs, fs, q, to_a, to_b = call(
                functools.partial(middle_kernel, away, first, power == ORDER, factor, step),
                [sds(16, 128), sds(64, 256), sds(16, 24, 128), sds(64, 128), sds(64, 128)],
                smem=2,
                scratch=edges + DIPOLE if away else edges,
                hbm=(2,) if away else (),
            )(*given)
        else:
            c, grid = call(
                functools.partial(last_kernel, factor, step),
                [sds(8, 128), sds(2, OWN, 512)],
                smem=2,
                scratch=(*DIPOLE, pltpu.SemaphoreType.DMA((2,))),
                hbm=(2, len(given)),
            )(*given, pltpu.with_memory_space_constraint(bulk, pltpu.HBM))
    return c.reshape(2, LB, 128), grid


def solution(mesh):
    placed = (
        P(None, "inner", "outer"),
        P(None, "inner", "outer"),
        P("inner", "outer"),
        P("inner", "outer", None),
        P("inner", None, "outer"),
        P("inner"),
        P("inner", None, None),
        P("inner", None, None),
        P("inner"),
        P(),
    )
    return jax.shard_map(
        local,
        mesh=mesh,
        in_specs=placed,
        out_specs=(P(None, "inner", "outer"), P(None, "inner", "outer")),
        check_vma=False,
    )
```
